512 devices in a mesh: lat: 64 (over x, y, z_hi), lon: 8 (over z_lo, core).
Axes of the slice: x: 4, y: 4, z: 16 (z_hi: 4, z_lo: 4; z = z_hi * 4 + z_lo), core: 2. Of those that a mesh axis runs over, the one named last changes fastest.
Arguments:
- velocity: float32 [2, 8, 512, 1024], P(None, None, 'lat', 'lon'), may hold values from -1.8 to 1.8
- thickness: float32 [8, 512, 1024], P(None, 'lat', 'lon'), may hold values from 0.5 to 1.5
- hydrography: float32 [2, 8, 512, 1024], P(None, None, 'lat', 'lon'), may hold values from -6 to 6
- tracers: float32 [17, 8, 512, 1024], P(None, None, 'lat', 'lon'), may hold values from -6 to 6
- land_mask: int32 [512, 1024], P('lat', 'lon'), may hold values 0 or 1
- bottom_layer: int32 [512, 1024], P('lat', 'lon'), may hold values from 1 to 8
- row_biome: int32 [512], P('lat'), may hold values from 0 to 3
- reaction_rates: float32 [17, 17], replicated, may hold values from -0.75 to 0.75
- growth_rates: float32 [4], replicated, may hold values from 0.2 to 2
Outputs:
- new_velocity: float32 [2, 8, 512, 1024], P(None, None, 'lat', 'lon')
- new_thickness: float32 [8, 512, 1024], P(None, 'lat', 'lon')
- new_hydrography: float32 [2, 8, 512, 1024], P(None, None, 'lat', 'lon')
- new_tracers: float32 [17, 8, 512, 1024], P(None, None, 'lat', 'lon')
- absorbed: float32 [8, 512, 1024], P(None, 'lat', 'lon')
The draws below stay inside these ranges and needn't reach their ends.
All inputs are finite; a program needn't handle non-finite values. No bound on the sum of `land_mask` on one device may be relied on, other than what follows from the above.
Results may differ from the reference program's by a relative error of at most 0.0003.
Values sent between devices are 32-bit elements; how exact they have to be, the bound alone decides.
No kernel may reach another device: no remote copies, remote signals or barrier semaphores. Data moves between devices by JAX's collectives and lax.ppermute only.
A program may use at most 64 MiB of HBM per device.

```python
import math
import jax
import jax.numpy as jnp
from jax import lax

NTR = 17
NBIOME = 4
NSUB = 2
K = 8
NY = 512
NX = 1024


def set_ends(drawn, key, least, high):
    index_at = [jax.random.randint(jax.random.fold_in(key, axis), (), 0, length) for axis, length in enumerate(drawn.shape)]
    longest = drawn.shape.index(max(drawn.shape))
    beside = index_at[:longest] + [(index_at[longest] + 1) % drawn.shape[longest]] + index_at[longest + 1:]
    return drawn.at[tuple(index_at)].set(least).at[tuple(beside)].set(high)


def block_levels(key, dims, pieces, smallest, high):
    factor_of, own = 1.0, jax.random.fold_in(key, 6)
    for position, shards_of in pieces:
        steps = jnp.exp(jax.random.uniform(jax.random.fold_in(own, position), (shards_of,), jnp.float32, smallest / len(pieces), high / len(pieces)))
        factor_of = factor_of * jnp.repeat(steps, dims[position] // shards_of).reshape([-1 if axis == position else 1 for axis in range(len(dims))])
    return factor_of


def gaussian(key, extent, scale, most, shards=(), dtype=jnp.bfloat16):
    drawn = scale * jax.random.normal(key, extent, jnp.float32)
    if shards:
        drawn = drawn * block_levels(key, extent, shards, -0.22, 0.18)
    return jnp.clip(drawn, -most, most).astype(dtype)


def setup_inputs(seed: int = 0) -> dict:
    splits = jax.random.split(jax.random.key(seed), 10)
    return {
        "velocity": gaussian(splits[0], (2, K, NY, NX), 0.3, 1.8, ((2, 64), (3, 8)), jnp.float32),
        "thickness": jnp.clip(0.5 + 1.0 * jax.random.uniform(splits[1], (K, NY, NX), jnp.float32) ** block_levels(splits[1], (K, NY, NX), ((1, 64), (2, 8)), -0.2, 0.2), 0.5, 1.5),
        "hydrography": gaussian(splits[2], (2, K, NY, NX), 1.0, 6.0, ((2, 64), (3, 8)), jnp.float32),
        "tracers": gaussian(splits[3], (NTR, K, NY, NX), 1.0, 6.0, ((2, 64), (3, 8)), jnp.float32),
        "land_mask": set_ends((jax.random.randint(splits[4], (NY, NX), 0, 4) < 3).astype(jnp.int32), jax.random.fold_in(splits[4], 1), 0, 1),
        "bottom_layer": set_ends(jax.random.randint(splits[5], (NY, NX), 1, K + 1), jax.random.fold_in(splits[5], 1), 1, K).astype(jnp.int32),
        "row_biome": set_ends(jax.random.randint(splits[6], (NY,), 0, NBIOME), jax.random.fold_in(splits[6], 1), 0, NBIOME - 1).astype(jnp.int32),
        "reaction_rates": gaussian(splits[7], (NTR, NTR), (4 * NTR) ** -0.5, 0.75, (), jnp.float32),
        "growth_rates": jnp.clip(jnp.exp(jax.random.uniform(splits[8], (NBIOME,), jnp.float32, math.log(0.2), math.log(2.0))), 0.2, 2.0),
    }


heat_coef = 0.2
salt_coef = 0.25
gravity = 0.3
viscosity = 0.1
coriolis_coef = 0.3
tracer_diff = 0.1
kappa_base = 0.02
kappa_var = 0.1
water_att = 0.1
chlorophyll_att = 0.2
heat_gain = 1.0


def shifted(values, step_rows, step_cols):
    leading = [(0, 0)] * (values.ndim - 2)
    padded = jnp.pad(values, leading + [(1, 1), (1, 1)])
    height_span = values.shape[-2]
    width_span = values.shape[-1]
    return padded[..., 1 + step_rows:1 + step_rows + height_span, 1 + step_cols:1 + step_cols + width_span]


def face_masks(wet_cells):
    return wet_cells * shifted(wet_cells, 0, 1), wet_cells * shifted(wet_cells, 1, 0)


def laplace(values, wet_east, wet_north):
    east_flux = wet_east * (shifted(values, 0, 1) - values)
    north_flux = wet_north * (shifted(values, 1, 0) - values)
    return east_flux - shifted(east_flux, 0, -1) + north_flux - shifted(north_flux, -1, 0)


def wet_layers(floor_depth, layers):
    layer_height = lax.broadcasted_iota(jnp.float32, (layers, 1, 1), 0)
    return (layer_height < floor_depth[None]).astype(jnp.float32)


def latitude_rows(start, count, total_rows):
    positions = start + lax.broadcasted_iota(jnp.float32, (count, 1), 0)
    return 2.0 * (positions + 0.5) / total_rows - 1.0


def density_of(hydrography):
    return salt_coef * hydrography[1] - heat_coef * hydrography[0]


def momentum(velocity, thickness, hydrography, wet_cells, coriolis):
    flow_east = velocity[0]
    flow_north = velocity[1]
    wet_east, wet_north = face_masks(wet_cells)
    pressure = gravity * thickness + density_of(hydrography)
    new_east = wet_east * (flow_east + coriolis * flow_north - (shifted(pressure, 0, 1) - pressure) + viscosity * laplace(flow_east, wet_east, wet_north))
    new_north = wet_north * (flow_north - coriolis * flow_east - (shifted(pressure, 1, 0) - pressure) + viscosity * laplace(flow_north, wet_east, wet_north))
    volume_east = wet_east * flow_east * 0.5 * (thickness + shifted(thickness, 0, 1))
    volume_north = wet_north * flow_north * 0.5 * (thickness + shifted(thickness, 1, 0))
    new_height = wet_cells * (thickness - (volume_east - shifted(volume_east, 0, -1) + volume_north - shifted(volume_north, -1, 0)))
    return new_east, new_north, new_height


def mixing(hydrography, wet_cells):
    density = density_of(hydrography)
    below = jnp.concatenate([density[1:] - density[:-1], jnp.zeros((1,) + density.shape[1:], jnp.float32)], 0)
    return wet_cells * (kappa_base + kappa_var / (1.0 + 10.0 * below * below))


def heat_salt(hydrography, wet_cells):
    wet_east, wet_north = face_masks(wet_cells)
    return wet_cells * (hydrography + tracer_diff * laplace(hydrography, wet_east, wet_north))


def light_field(tracers, wet_cells, insolation):
    chlorophyll = tracers[1]
    attenuation = wet_cells * (water_att + chlorophyll_att * chlorophyll * chlorophyll)
    overhead = jnp.cumsum(attenuation, axis=0) - attenuation
    top_light = insolation * jnp.exp(-overhead)
    return top_light, top_light * (1.0 - jnp.exp(-attenuation))


def tracer_step(tracers, flow_east, flow_north, thickness, kappa, wet_cells, reaction_rates, growth_field, top_light):
    sub_step = 1.0 / NSUB
    wet_east, wet_north = face_masks(wet_cells)
    transport_x = wet_east * flow_east * 0.5 * (thickness + shifted(thickness, 0, 1))
    transport_y = wet_north * flow_north * 0.5 * (thickness + shifted(thickness, 1, 0))
    diffuse_x = wet_east * 0.5 * (kappa + shifted(kappa, 0, 1))
    diffuse_y = wet_north * 0.5 * (kappa + shifted(kappa, 1, 0))
    east_next = shifted(tracers, 0, 1)
    north_next = shifted(tracers, 1, 0)
    flux_x = transport_x * jnp.where(transport_x > 0, tracers, east_next) - diffuse_x * (east_next - tracers)
    flux_y = transport_y * jnp.where(transport_y > 0, tracers, north_next) - diffuse_y * (north_next - tracers)
    advected = tracers - sub_step * (flux_x - shifted(flux_x, 0, -1) + flux_y - shifted(flux_y, -1, 0))
    flattened = advected.reshape(advected.shape[0], -1)
    coupled = jnp.dot(reaction_rates, flattened, precision=lax.Precision.HIGHEST).reshape(advected.shape)
    nutrient = advected[0]
    plankton = advected[1]
    uptake = growth_field * top_light * plankton * nutrient * nutrient / (1.0 + nutrient * nutrient)
    change = jnp.concatenate([(coupled[0] - uptake)[None], (coupled[1] + uptake)[None], coupled[2:]], 0)
    return wet_cells * (advected + sub_step * change)


def reference(velocity, thickness, hydrography, tracers, land_mask, bottom_layer, row_biome, reaction_rates, growth_rates):
    floor_depth = (land_mask * bottom_layer).astype(jnp.float32)
    wet_cells = wet_layers(floor_depth, K)
    latitude = latitude_rows(jnp.float32(0.0), NY, NY)
    insolation = 1.0 - 0.8 * latitude * latitude
    coriolis = coriolis_coef * latitude
    top_light, absorbed = light_field(tracers, wet_cells, insolation)
    new_east, new_north, new_height = momentum(velocity, thickness, hydrography, wet_cells, coriolis)
    kappa = mixing(hydrography, wet_cells)
    mixed = heat_salt(hydrography, wet_cells)
    new_hydrography = jnp.concatenate([(mixed[0] + heat_gain * absorbed)[None], mixed[1:]], 0)
    biome_table = (row_biome[:, None] == lax.broadcasted_iota(jnp.int32, (1, NBIOME), 1)).astype(jnp.float32)
    growth_field = jnp.dot(biome_table, growth_rates[:, None], precision=lax.Precision.HIGHEST)
    current = tracers
    for substep in range(NSUB):
        current = tracer_step(current, new_east, new_north, new_height, kappa, wet_cells, reaction_rates, growth_field, top_light)
    return jnp.stack([new_east, new_north]), new_height, new_hydrography, current, absorbed
```

```python
import jax
import jax.numpy as jnp
from jax import lax
from jax.experimental import pallas as pl
from jax.experimental.pallas import tpu as pltpu
from jax.sharding import PartitionSpec as P

F32 = jnp.float32
NSUB = 2
SUB = 1.0 / NSUB
NTR = 17
K = 8
ROWS = 8
COLS = 128
FU, FV, FH, FT, FS, FD = 17, 18, 19, 20, 21, 22
NF = 24
PAIRS = NF // 2
B_A, B_B, B_DA, B_DB, B_C = 0, 17, 34, 39, 44
N_FWD, N_BWD = 47, 46


def lanes(shape):
    return lax.broadcasted_iota(jnp.int32, shape, len(shape) - 1)


def subs(shape):
    return lax.broadcasted_iota(jnp.int32, shape, len(shape) - 2)


def growth_of(biome_ref, rates_ref, row):
    kind = biome_ref[row]
    rate = rates_ref[0]
    for i in range(1, rates_ref.shape[0]):
        rate = jnp.where(kind == i, rates_ref[i], rate)
    return rate


def depth_of(land_ref, bottom_ref):
    return (land_ref[...] * bottom_ref[...]).astype(F32)


def layer_rows(ref, plane, row):
    return ref[pl.ds(plane * ROWS + row, K, stride=ROWS), :]


def lat_pack(vel, thk, hyd, trc, land, bottom, biome, rates, fwd, bwd):
    depth = depth_of(land, bottom)
    sub = subs((ROWS, COLS))

    def put(out, block, value):
        out[pl.ds(block * K, K), :] = value

    def state(out, block, row):
        put(out, block, layer_rows(vel, 0, row))
        put(out, block + 1, layer_rows(vel, K, row))
        put(out, block + 2, layer_rows(thk, 0, row))
        put(out, block + 3, layer_rows(hyd, 0, row))
        put(out, block + 4, layer_rows(hyd, K, row))

    for out, a, b in ((fwd, ROWS - 1, ROWS - 2), (bwd, 0, 1)):
        for t in range(NTR):
            put(out, B_A + t, layer_rows(trc, t * K, a))
            put(out, B_B + t, layer_rows(trc, t * K, b))
        state(out, B_DA, a)
        state(out, B_DB, b)
    put(fwd, B_C, layer_rows(vel, K, ROWS - 3))
    put(fwd, B_C + 1, layer_rows(thk, 0, ROWS - 3))
    put(bwd, B_C, layer_rows(thk, 0, 2))
    put(fwd, N_FWD - 1, jnp.where(sub == 3, growth_of(biome, rates, ROWS - 1), depth))
    put(bwd, N_BWD - 1, jnp.where(sub == 3, growth_of(biome, rates, 0), depth))


def lon_pack(vel, thk, hyd, trc, land, bottom, out):
    depth = depth_of(land, bottom)
    group = lanes((ROWS, COLS)) >> 3

    def plane(f, k):
        if f < NTR:
            return trc[pl.ds((f * K + k) * ROWS, ROWS), :]
        if f < FH:
            return vel[pl.ds(((f - FU) * K + k) * ROWS, ROWS), :]
        if f == FH:
            return thk[pl.ds(k * ROWS, ROWS), :]
        if f < FD:
            return hyd[pl.ds(((f - FT) * K + k) * ROWS, ROWS), :]
        return depth

    for p in range(PAIRS):
        packed = jnp.zeros((ROWS, COLS), F32)
        for half in range(2):
            f = p + PAIRS * half
            if f > FD:
                continue
            for k in range(K):
                moved = pltpu.roll(plane(f, k), (half * 64 + (7 - k) * 8 + 4) % COLS, 1)
                packed = jnp.where(group == half * 8 + 7 - k, moved, packed)
        out[pl.ds(p * ROWS, ROWS), :] = packed


def edge_pack(own, west, east, edge, fwd, bwd):
    lane = lanes((ROWS, COLS))
    low = (lane & 7) < 4
    left = lane < 64
    for p in range(PAIRS):
        at = pl.ds(p * ROWS, ROWS)
        o = own[at, :]
        x = jnp.where(low, west[at, :], o)
        y = jnp.where(low, o, east[at, :])
        edge[pl.ds(p * ROWS, ROWS), :] = jnp.where(left, x, pltpu.roll(y, 64, 1))
        edge[pl.ds((p + PAIRS) * ROWS, ROWS), :] = jnp.where(left, pltpu.roll(x, 64, 1), y)
    for out, a, b, c in ((fwd, 7, 6, 5), (bwd, 0, 1, 2)):
        for i in range(3):
            out[pl.ds(i * 8, 8), :] = edge[pl.ds(i * 64 + a, 8, stride=8), :]
        out[pl.ds(24, 8), :] = edge[pl.ds(128 + b, 8, stride=8), :]
        out[pl.ds(32, 8), :] = edge[pl.ds(128 + c, 8, stride=8), :]


def kappa_of(wet, below):
    return wet * (0.02 + 0.1 / (1.0 + 10.0 * below * below))


def density(t, s):
    return 0.25 * s - 0.2 * t


def laplace(a, ae, aw, an, as_, we, ww, wn, ws):
    return we * (ae - a) - ww * (a - aw) + wn * (an - a) - ws * (a - as_)


def parts(transport, diffuse):
    return jnp.maximum(transport, 0.0) + diffuse, jnp.minimum(transport, 0.0) - diffuse


def step_weights(te, de, tw, dw, tn, dn, ts, ds):
    ae, be = parts(te, de)
    aw, bw = parts(tw, dw)
    an, bn = parts(tn, dn)
    as_, bs = parts(ts, ds)
    return 1.0 - SUB * (ae - bw + an - bs), -SUB * be, SUB * aw, -SUB * bn, SUB * as_


def react(adv, rate_at, wet, gain, store):
    nutrient = adv[0]
    square = nutrient * nutrient
    uptake = gain * adv[1] * square / (1.0 + square)
    for t in range(NTR):
        total = adv[t]
        for s in range(NTR):
            total = total + rate_at(t, s) * adv[s]
        if t == 0:
            total = total - uptake
        if t == 1:
            total = total + uptake
        store(t, wet * total)


def step(total_rows, vel, thk, hyd, trc, land, bottom, biome, rates, rr, lat_s, lat_n, edge, cor_s, cor_n,
         out_vel, out_thk, out_hyd, out_trc, out_abs,
         ex, es, mp, l1s, l1n, lw, c1, cf, half_rate):
    first = (lax.axis_index("lat") * ROWS).astype(F32)

    def latitude(row):
        return 2.0 * (first + row + 0.5) / total_rows - 1.0

    for t in range(NTR):
        for s in range(NTR):
            half_rate[t * NTR + s] = SUB * rr[t, s]

    def rate_at(t, s):
        return half_rate[t * NTR + s]

    lane = lanes((ROWS, COLS))
    sub = subs((ROWS, COLS))
    at_first, at_last = lane == 0, lane == COLS - 1
    top_row, end_row = sub == 0, sub == ROWS - 1

    def mprime(value):
        return jnp.where((lane & 7) == 5, pltpu.roll(value, 2, 1), pltpu.roll(value, 64, 1))

    for f in range(NF - 1):
        own = edge[pl.ds(f * ROWS, ROWS), :]
        mp[f] = mprime(own)
        if f >= NTR:
            ex[f, 0:8, :] = jnp.zeros((8, COLS), F32)
            ex[f, 16:24, :] = jnp.zeros((8, COLS), F32)
            for i, at in ((1, 24), (2, 32)):
                ex[f, 7 - i:8 - i, :] = cor_s[at + f - 16:at + f - 15, :]
                ex[f, 16 + i:17 + i, :] = cor_n[at + f - 16:at + f - 15, :]
        ex[f, 7:8, :] = cor_s[f:f + 1, :]
        ex[f, 16:17, :] = cor_n[f:f + 1, :]
        ex[f, 8:16, :] = own

    def east(a):
        return pltpu.roll(a, COLS - 1, 1)

    def west(a):
        return pltpu.roll(a, 1, 1)

    def north(a):
        return pltpu.roll(a, 23, 0)

    def south(a):
        return pltpu.roll(a, 1, 0)

    big = (24, COLS)
    layer = 7 - ((lanes(big) >> 3) & 7)
    u, v, h, t_, s_ = ex[FU], ex[FV], ex[FH], ex[FT], ex[FS]
    wet = (layer.astype(F32) < ex[FD]).astype(F32)
    rho = density(t_, s_)
    p = 0.3 * h + rho
    cor = 0.3 * latitude((subs(big) - 8).astype(F32))
    we = wet * east(wet)
    wn = wet * north(wet)
    ww, ws = west(we), south(wn)
    lap_u = laplace(u, east(u), west(u), north(u), south(u), we, ww, wn, ws)
    lap_v = laplace(v, east(v), west(v), north(v), south(v), we, ww, wn, ws)
    new_u = we * (u + cor * v - (east(p) - p) + 0.1 * lap_u)
    new_v = wn * (v - cor * u - (north(p) - p) + 0.1 * lap_v)
    qe = we * u * 0.5 * (h + east(h))
    qn = wn * v * 0.5 * (h + north(h))
    new_h = wet * (h - (qe - west(qe) + qn - south(qn)))
    kap = kappa_of(wet, jnp.where(layer < K - 1, pltpu.roll(rho, 8, 1) - rho, 0.0))
    te = new_u * 0.5 * (new_h + east(new_h))
    tn = new_v * 0.5 * (new_h + north(new_h))
    de = we * 0.5 * (kap + east(kap))
    dn = wn * 0.5 * (kap + north(kap))
    for i, value in enumerate((new_h, kap, te, de)):
        es[i] = value
        mp[FD + 1 + i] = mprime(value[8:16])
    weights = step_weights(te, de, west(te), west(de), tn, dn, south(tn), south(dn))
    weights = [w[8:16] for w in weights]
    small_layer = 7 - ((lane >> 3) & 7)
    wet8 = wet[8:16]
    chl = ex[1, 8:16, :]
    att = wet8 * (0.1 + 0.2 * chl * chl)
    total = att
    for shift in (1, 2, 4):
        total = total + jnp.where(small_layer >= shift, pltpu.roll(total, COLS - 8 * shift, 1), 0.0)
    lat8 = latitude(sub.astype(F32))
    sun8 = 1.0 - 0.8 * lat8 * lat8
    grow8 = jnp.zeros((ROWS, COLS), F32)
    for r in range(ROWS):
        grow8 = jnp.where(sub == r, growth_of(biome, rates, r), grow8)
    gain = SUB * grow8 * sun8 * jnp.exp(-(total - att))
    adv = []
    for t in range(NTR):
        c = ex[t, 8:16, :]
        w0, w1, w2, w3, w4 = weights
        adv.append(w0 * c + w1 * east(c) + w2 * west(c) + w3 * ex[t, 9:17, :] + w4 * ex[t, 7:15, :])

    def keep_edge(t, value):
        mp[NF + 4 + t] = mprime(value)

    react(adv, rate_at, wet8, gain, keep_edge)

    def layered(row):
        return jnp.broadcast_to(row, (K, COLS))

    def from_west(row):
        return pltpu.roll(layered(row), 69, 1, stride=8, stride_axis=0)

    def from_east(row):
        return pltpu.roll(layered(row), 3, 1, stride=8, stride_axis=0)

    def lat_east(a, row):
        return jnp.where(at_last, from_east(row), east(a))

    def lat_west(a, row):
        return jnp.where(at_first, from_west(row), west(a))

    kf = sub.astype(F32)
    own_depth = depth_of(land, bottom)
    mp_depth = own_depth
    lw[0] = mp_depth

    def block(ref, i):
        return ref[pl.ds(i * K, K), :]

    class Line:
        pass

    def line(ref, misc, base, er, depth_row):
        o = Line()
        o.u, o.v, o.h, o.t, o.s = (block(ref, base + i) for i in range(5))
        o.wet = (kf < layered(ref[misc * K + depth_row:misc * K + depth_row + 1, :])).astype(F32)
        o.er = er
        return around(o)

    def around(o):
        er = o.er
        o.p = 0.3 * o.h + density(o.t, o.s)

        def e(f):
            return ex[f, er:er + 1, :]

        o.ue, o.uw = lat_east(o.u, e(FU)), lat_west(o.u, e(FU))
        o.ve, o.vw = lat_east(o.v, e(FV)), lat_west(o.v, e(FV))
        o.he, o.hw = lat_east(o.h, e(FH)), lat_west(o.h, e(FH))
        pe = 0.3 * e(FH) + density(e(FT), e(FS))
        o.pe = lat_east(o.p, pe)
        wet_e = (kf < from_east(e(FD))).astype(F32)
        wet_w = (kf < from_west(e(FD))).astype(F32)
        o.we = o.wet * jnp.where(at_last, wet_e, east(o.wet))
        o.ww = o.wet * jnp.where(at_first, wet_w, west(o.wet))
        rho = density(o.t, o.s)
        o.kap = kappa_of(o.wet, jnp.where(sub < K - 1, pltpu.roll(rho, K - 1, 0) - rho, 0.0))
        return o

    def own_line(row):
        o = Line()
        o.u, o.v, o.h = layer_rows(vel, 0, row), layer_rows(vel, K, row), layer_rows(thk, 0, row)
        o.p = 0.3 * o.h + density(layer_rows(hyd, 0, row), layer_rows(hyd, K, row))
        o.wet = (kf < layered(lw[0, row:row + 1, :])).astype(F32)
        return o

    def height(o, n, s):
        wn, ws = o.wet * n.wet, o.wet * s.wet
        qe = o.we * o.u * 0.5 * (o.h + o.he)
        qw = o.ww * o.uw * 0.5 * (o.hw + o.h)
        qn = wn * o.v * 0.5 * (o.h + n.h)
        qs = ws * s.v * 0.5 * (s.h + o.h)
        return o.wet * (o.h - (qe - qw + qn - qs))

    def east_speed(o, n, s, cor):
        wn, ws = o.wet * n.wet, o.wet * s.wet
        return o.we * (o.u + cor * o.v - (o.pe - o.p) + 0.1 * laplace(o.u, o.ue, o.uw, n.u, s.u, o.we, o.ww, wn, ws))

    def north_speed(o, n, s, cor):
        wn, ws = o.wet * n.wet, o.wet * s.wet
        return wn * (o.v - cor * o.u - (n.p - o.p) + 0.1 * laplace(o.v, o.ve, o.vw, n.v, s.v, o.we, o.ww, wn, ws))

    sa = line(lat_s, N_FWD - 1, B_DA, 7, 7)
    sb = line(lat_s, N_FWD - 1, B_DB, 6, 6)
    sc = Line()
    sc.v, sc.h = block(lat_s, B_C), block(lat_s, B_C + 1)
    sc.wet = (kf < layered(lat_s[(N_FWD - 1) * K + 5:(N_FWD - 1) * K + 6, :])).astype(F32)
    na = line(lat_n, N_BWD - 1, B_DA, 16, 0)
    nb = line(lat_n, N_BWD - 1, B_DB, 17, 1)
    nc = Line()
    nc.h = block(lat_n, B_C)
    nc.wet = (kf < layered(lat_n[(N_BWD - 1) * K + 2:(N_BWD - 1) * K + 3, :])).astype(F32)
    row0, row7 = own_line(0), own_line(ROWS - 1)

    sa.nu = east_speed(sa, row0, sb, 0.3 * latitude(-1.0))
    sa.nv = north_speed(sa, row0, sb, 0.3 * latitude(-1.0))
    sa.nh = height(sa, row0, sb)
    sb.nv = north_speed(sb, sa, sc, 0.3 * latitude(-2.0))
    sb.nh = height(sb, sa, sc)
    na.nu = east_speed(na, nb, row7, 0.3 * latitude(float(ROWS)))
    na.nv = north_speed(na, nb, row7, 0.3 * latitude(float(ROWS)))
    na.nh = height(na, nb, row7)
    nb.nh = height(nb, nc, na)
    for i, value in enumerate((sa.nv, sa.nh, sa.kap, na.nh, na.kap)):
        lw[1 + i] = value

    lat_col = latitude(sub.astype(F32))
    cor8 = 0.3 * lat_col
    depth_mp = mp[FD]

    def row_of(ref, at):
        return jnp.broadcast_to(ref[pl.ds(at, 1), :], (ROWS, COLS))

    def around_sides(value, f, shift):
        edge_value = pltpu.roll(mp[f], shift, 1)
        return jnp.where(at_last, edge_value, east(value)), jnp.where(at_first, edge_value, west(value))

    def around_ends(value, rn, rs):
        return jnp.where(end_row, rn, pltpu.roll(value, ROWS - 1, 0)), jnp.where(top_row, rs, pltpu.roll(value, 1, 0))

    dep_e, dep_w = around_sides(own_depth, FD, 67)
    dep_n, dep_s = around_ends(own_depth, row_of(lat_n, (N_BWD - 1) * K), row_of(lat_s, (N_FWD - 1) * K + 7))

    def cells(k, over):
        shift = 67 + 8 * k
        kk = k.astype(F32)
        at = pl.ds(pl.multiple_of(k * ROWS, ROWS), ROWS)
        at2 = pl.ds(pl.multiple_of((k + K) * ROWS, ROWS), ROWS)
        u, v, h, t_, s_ = vel[at, :], vel[at2, :], thk[at, :], hyd[at, :], hyd[at2, :]
        wet = (kk < own_depth).astype(F32)
        we = wet * (kk < dep_e).astype(F32)
        ww = wet * (kk < dep_w).astype(F32)
        wn = wet * (kk < dep_n).astype(F32)
        ws = wet * (kk < dep_s).astype(F32)

        def near(value, f, i):
            e, w = around_sides(value, f, shift)
            n, s = around_ends(value, row_of(lat_n, (B_DA + i) * K + k), row_of(lat_s, (B_DA + i) * K + k))
            return e, w, n, s

        ue, uw, un, us = near(u, FU, 0)
        ve, vw, vn, vs = near(v, FV, 1)
        he, hw, hn, hs = near(h, FH, 2)
        t_e, tw, t_n, ts = near(t_, FT, 3)
        s_e, sw, s_n, ss = near(s_, FS, 4)
        p = 0.3 * h + density(t_, s_)
        pe = 0.3 * he + density(t_e, s_e)
        pn = 0.3 * hn + density(t_n, s_n)
        nu = we * (u + cor8 * v - (pe - p) + 0.1 * laplace(u, ue, uw, un, us, we, ww, wn, ws))
        nv = wn * (v - cor8 * u - (pn - p) + 0.1 * laplace(v, ve, vw, vn, vs, we, ww, wn, ws))
        qe = we * u * 0.5 * (h + he)
        qw = ww * uw * 0.5 * (hw + h)
        qn = wn * v * 0.5 * (h + hn)
        qs = ws * vs * 0.5 * (hs + h)
        nh = wet * (h - (qe - qw + qn - qs))
        out_vel[at, :] = nu
        out_vel[at2, :] = nv
        out_thk[at, :] = nh
        lower = jnp.minimum(k + 1, K - 1)
        al = pl.ds(pl.multiple_of(lower * ROWS, ROWS), ROWS)
        al2 = pl.ds(pl.multiple_of((lower + K) * ROWS, ROWS), ROWS)
        below = density(hyd[al, :], hyd[al2, :]) - density(t_, s_)
        kap = kappa_of(wet, below)
        chl = trc[pl.ds(pl.multiple_of((k + K) * ROWS, ROWS), ROWS), :]
        att = wet * (0.1 + 0.2 * chl * chl)
        light = sun8 * jnp.exp(-over)
        absorbed = light * (1.0 - jnp.exp(-att))
        out_abs[at, :] = absorbed
        out_hyd[at, :] = wet * (t_ + 0.1 * laplace(t_, t_e, tw, t_n, ts, we, ww, wn, ws)) + absorbed
        out_hyd[at2, :] = wet * (s_ + 0.1 * laplace(s_, s_e, sw, s_n, ss, we, ww, wn, ws))
        nhe = jnp.where(at_last, pltpu.roll(mp[FD + 1], shift, 1), east(nh))
        kape = jnp.where(at_last, pltpu.roll(mp[FD + 2], shift, 1), east(kap))
        nhn = jnp.where(end_row, row_of(lw.at[4], k), pltpu.roll(nh, ROWS - 1, 0))
        kapn = jnp.where(end_row, row_of(lw.at[5], k), pltpu.roll(kap, ROWS - 1, 0))
        te = nu * 0.5 * (nh + nhe)
        de = we * 0.5 * (kap + kape)
        tn = nv * 0.5 * (nh + nhn)
        dn = wn * 0.5 * (kap + kapn)
        tw = jnp.where(at_first, pltpu.roll(mp[FD + 3], shift, 1), west(te))
        dw = jnp.where(at_first, pltpu.roll(mp[FD + 4], shift, 1), west(de))
        ts = jnp.where(top_row, row_of(lw.at[1], k) * 0.5 * (row_of(lw.at[2], k) + nh), pltpu.roll(tn, 1, 0))
        ds = jnp.where(top_row, ws * 0.5 * (row_of(lw.at[3], k) + kap), pltpu.roll(dn, 1, 0))
        for i, w in enumerate(step_weights(te, de, tw, dw, tn, dn, ts, ds)):
            cf[i, at, :] = w
        cf[5, at, :] = SUB * grow8 * light
        cf[6, at, :] = tn
        cf[7, at, :] = dn
        return over + att

    lax.fori_loop(0, K, cells, jnp.zeros((ROWS, COLS), F32))

    def outer(o, te_row, grow, lat_row, tn, dn, ts, ds, near_ref, north_of, south_of, er, kept):
        he = lat_east(o.nh, es[0, er:er + 1, :])
        kape = lat_east(o.kap, es[1, er:er + 1, :])
        te = o.nu * 0.5 * (o.nh + he)
        de = o.we * 0.5 * (o.kap + kape)
        tw = lat_west(te, es[2, er:er + 1, :])
        dw = lat_west(de, es[3, er:er + 1, :])
        w0, w1, w2, w3, w4 = step_weights(te, de, tw, dw, tn, dn, ts, ds)
        chl = block(near_ref, B_A + 1)
        att = o.wet * (0.1 + 0.2 * chl * chl)
        total = att
        for shift in (1, 2, 4):
            total = total + jnp.where(sub >= shift, pltpu.roll(total, shift, 0), 0.0)
        lat_here = latitude(lat_row)
        gain = SUB * layered(grow) * ((1.0 - 0.8 * lat_here * lat_here) * jnp.exp(-(total - att)))
        adv = []
        for t in range(NTR):
            c = block(near_ref, B_A + t)
            row = ex[t, er:er + 1, :]
            adv.append(w0 * c + w1 * lat_east(c, row) + w2 * lat_west(c, row) + w3 * north_of(t) + w4 * south_of(t))

        def keep(t, value):
            kept[pl.ds(t * K, K), :] = value

        react(adv, rate_at, o.wet, gain, keep)

    h0 = layer_rows(out_thk, 0, 0)
    kap0 = kappa_of(row0.wet, row_below(hyd, 0, sub))
    wn_s = sa.wet * row0.wet
    outer(sa, None, lat_s[(N_FWD - 1) * K + 3:(N_FWD - 1) * K + 4, :], -1.0,
          sa.nv * 0.5 * (sa.nh + h0), wn_s * 0.5 * (sa.kap + kap0),
          sb.nv * 0.5 * (sb.nh + sa.nh), sb.wet * sa.wet * 0.5 * (sb.kap + sa.kap),
          lat_s, lambda t: layer_rows(trc, t * K, 0), lambda t: block(lat_s, B_B + t), 7, l1s)
    outer(na, None, lat_n[(N_BWD - 1) * K + 3:(N_BWD - 1) * K + 4, :], float(ROWS),
          na.nv * 0.5 * (na.nh + nb.nh), na.wet * nb.wet * 0.5 * (na.kap + nb.kap),
          layer_rows(cf.at[6], 0, ROWS - 1), layer_rows(cf.at[7], 0, ROWS - 1),
          lat_n, lambda t: block(lat_n, B_B + t), lambda t: layer_rows(trc, t * K, ROWS - 1), 16, l1n)

    def substep(src, dst, mp_base, end_n, end_s):
        def body(k, carry):
            shift = 67 + 8 * k
            at = pl.ds(pl.multiple_of(k * ROWS, ROWS), ROWS)
            w0, w1, w2, w3, w4 = (cf[i, at, :] for i in range(5))
            wet = (k.astype(F32) < own_depth).astype(F32)
            adv = []
            for t in range(NTR):
                c = src[pl.ds(pl.multiple_of((t * K + k) * ROWS, ROWS), ROWS), :]
                e, w = around_sides(c, mp_base + t, shift)
                n, s = around_ends(c, row_of(end_n, t * K + k), row_of(end_s, t * K + k))
                adv.append(w0 * c + w1 * e + w2 * w + w3 * n + w4 * s)

            def keep(t, value):
                dst[pl.ds(pl.multiple_of((t * K + k) * ROWS, ROWS), ROWS), :] = value

            react(adv, rate_at, wet, cf[5, at, :], keep)
            return carry

        lax.fori_loop(0, K, body, 0)

    substep(trc, c1, 0, lat_n, lat_s)
    substep(c1, out_trc, NF + 4, l1n, l1s)


def row_below(hyd, row, sub):
    rho = density(layer_rows(hyd, 0, row), layer_rows(hyd, K, row))
    return jnp.where(sub < K - 1, pltpu.roll(rho, K - 1, 0) - rho, 0.0)


def shape(*dims):
    return jax.ShapeDtypeStruct(dims, F32)


def call(kernel, out_shape, n_vmem, n_smem, after=0, scratch=(), flops=100000):
    vmem = pl.BlockSpec(memory_space=pltpu.VMEM)
    smem = pl.BlockSpec(memory_space=pltpu.SMEM)
    return pl.pallas_call(
        kernel,
        out_shape=out_shape,
        in_specs=[vmem] * n_vmem + [smem] * n_smem + [vmem] * after,
        out_specs=jax.tree.map(lambda _: vmem, out_shape),
        scratch_shapes=list(scratch),
        cost_estimate=pl.CostEstimate(flops=flops, bytes_accessed=100000, transcendentals=0),
    )


def per_device(velocity, thickness, hydrography, tracers, land_mask, bottom_layer, row_biome, reaction_rates, growth_rates):
    lat, lon = lax.axis_size("lat"), lax.axis_size("lon")
    vel = velocity.reshape(2 * K * ROWS, COLS)
    thk = thickness.reshape(K * ROWS, COLS)
    hyd = hydrography.reshape(2 * K * ROWS, COLS)
    trc = tracers.reshape(NTR * K * ROWS, COLS)
    up = lambda n: [(i, i + 1) for i in range(n - 1)]
    down = lambda n: [(i + 1, i) for i in range(n - 1)]

    fwd, bwd = call(lat_pack, (shape(N_FWD * K, COLS), shape(N_BWD * K, COLS)), 6, 2)(
        vel, thk, hyd, trc, land_mask, bottom_layer, row_biome, growth_rates)
    lat_s = lax.ppermute(fwd, "lat", up(lat))
    lat_n = lax.ppermute(bwd, "lat", down(lat))
    own = call(lon_pack, shape(PAIRS * ROWS, COLS), 6, 0)(vel, thk, hyd, trc, land_mask, bottom_layer)
    from_west = lax.ppermute(own, "lon", up(lon))
    from_east = lax.ppermute(own, "lon", down(lon))
    edge, cfwd, cbwd = call(edge_pack, (shape(NF * ROWS, COLS), shape(40, COLS), shape(40, COLS)), 3, 0)(
        own, from_west, from_east)
    cor_s = lax.ppermute(cfwd, "lat", up(lat))
    cor_n = lax.ppermute(cbwd, "lat", down(lat))

    def body(*refs):
        step(lat * ROWS, *refs)

    outs = call(
        body,
        (shape(2 * K * ROWS, COLS), shape(K * ROWS, COLS), shape(2 * K * ROWS, COLS), shape(NTR * K * ROWS, COLS), shape(K * ROWS, COLS)),
        6, 3, after=5,
        scratch=[
            pltpu.VMEM((NF, 24, COLS), F32),
            pltpu.VMEM((4, 24, COLS), F32),
            pltpu.VMEM((NF + 4 + NTR, ROWS, COLS), F32),
            pltpu.VMEM((NTR * K, COLS), F32),
            pltpu.VMEM((NTR * K, COLS), F32),
            pltpu.VMEM((6, ROWS, COLS), F32),
            pltpu.VMEM((NTR * K * ROWS, COLS), F32),
            pltpu.VMEM((8, K * ROWS, COLS), F32),
            pltpu.SMEM((NTR * NTR,), F32),
        ],
    )(vel, thk, hyd, trc, land_mask, bottom_layer, row_biome, growth_rates, reaction_rates, lat_s, lat_n, edge, cor_s, cor_n)
    new_vel, new_thk, new_hyd, new_trc, absorbed = outs
    return (new_vel.reshape(velocity.shape), new_thk.reshape(thickness.shape), new_hyd.reshape(hydrography.shape),
            new_trc.reshape(tracers.shape), absorbed.reshape(thickness.shape))


def solution(mesh):
    field = P(None, "lat", "lon")
    fields = P(None, None, "lat", "lon")
    in_specs = (fields, field, fields, fields, P("lat", "lon"), P("lat", "lon"), P("lat"), P(), P())
    out_specs = (fields, field, fields, fields, field)
    return jax.shard_map(per_device, mesh=mesh, in_specs=in_specs, out_specs=out_specs, check_vma=False)
```

```python
import jax
import jax.numpy as jnp
from jax import lax
from jax.experimental import pallas as pl
from jax.experimental.pallas import tpu as pltpu
from jax.sharding import PartitionSpec as P

F32 = jnp.float32
NSUB = 2
SUB = 1.0 / NSUB
NTR = 17
K = 8
ROWS = 8
COLS = 128
FU, FV, FH, FT, FS, FD = 17, 18, 19, 20, 21, 22
NF = 24
PAIRS = NF // 2
B_A, B_B, B_DA, B_DB, B_C = 0, 17, 34, 39, 44
N_FWD, N_BWD = 47, 46
C_FWD, C_BWD = N_FWD * K, N_BWD * K
ROWS_FWD, ROWS_BWD = C_FWD + 40, C_BWD + 40


def lanes(shape):
    return lax.broadcasted_iota(jnp.int32, shape, len(shape) - 1)


def subs(shape):
    return lax.broadcasted_iota(jnp.int32, shape, len(shape) - 2)


def growth_of(biome_ref, rates_ref, row):
    kind = biome_ref[row]
    rate = rates_ref[0]
    for i in range(1, rates_ref.shape[0]):
        rate = jnp.where(kind == i, rates_ref[i], rate)
    return rate


def depth_of(land_ref, bottom_ref):
    return (land_ref[...] * bottom_ref[...]).astype(F32)


def layer_rows(ref, plane, row):
    return ref[pl.ds(plane * ROWS + row, K, stride=ROWS), :]


def lat_pack(vel, thk, hyd, trc, land, bottom, after, biome, rates, fwd, bwd):
    depth = depth_of(land, bottom)
    sub = subs((ROWS, COLS))

    def put(out, block, value):
        out[pl.ds(block * K, K), :] = value

    def state(out, block, row):
        put(out, block, layer_rows(vel, 0, row))
        put(out, block + 1, layer_rows(vel, K, row))
        put(out, block + 2, layer_rows(thk, 0, row))
        put(out, block + 3, layer_rows(hyd, 0, row))
        put(out, block + 4, layer_rows(hyd, K, row))

    for out, a, b in ((fwd, ROWS - 1, ROWS - 2), (bwd, 0, 1)):
        for t in range(NTR):
            put(out, B_A + t, layer_rows(trc, t * K, a))
            put(out, B_B + t, layer_rows(trc, t * K, b))
        state(out, B_DA, a)
        state(out, B_DB, b)
    put(fwd, B_C, layer_rows(vel, K, ROWS - 3))
    put(fwd, B_C + 1, layer_rows(thk, 0, ROWS - 3))
    put(bwd, B_C, layer_rows(thk, 0, 2))
    put(fwd, N_FWD - 1, jnp.where(sub == 3, growth_of(biome, rates, ROWS - 1), depth))
    put(bwd, N_BWD - 1, jnp.where(sub == 3, growth_of(biome, rates, 0), depth))


def lon_pack(vel, thk, hyd, trc, land, bottom, out):
    depth = depth_of(land, bottom)
    group = lanes((ROWS, COLS)) >> 3

    def plane(f, k):
        if f < NTR:
            return trc[pl.ds((f * K + k) * ROWS, ROWS), :]
        if f < FH:
            return vel[pl.ds(((f - FU) * K + k) * ROWS, ROWS), :]
        if f == FH:
            return thk[pl.ds(k * ROWS, ROWS), :]
        if f < FD:
            return hyd[pl.ds(((f - FT) * K + k) * ROWS, ROWS), :]
        return depth

    for p in range(PAIRS):
        packed = jnp.zeros((ROWS, COLS), F32)
        for half in range(2):
            f = p + PAIRS * half
            if f > FD:
                continue
            for k in range(K):
                moved = pltpu.roll(plane(f, k), (half * 64 + (7 - k) * 8 + 4) % COLS, 1)
                packed = jnp.where(group == half * 8 + 7 - k, moved, packed)
        out[pl.ds(p * ROWS, ROWS), :] = packed


def edge_pack(own, inner, outer, fwd_in, bwd_in, edge, fwd, bwd):
    lane = lanes((ROWS, COLS))
    low = (lane & 7) < 4
    left = lane < 64
    odd = jnp.full((ROWS, COLS), lax.axis_index("lon") & 1) == 1
    for p in range(PAIRS):
        at = pl.ds(p * ROWS, ROWS)
        o, a, b = own[at, :], inner[at, :], outer[at, :]
        x = jnp.where(low, jnp.where(odd, a, b), o)
        y = jnp.where(low, o, jnp.where(odd, b, a))
        edge[pl.ds(p * ROWS, ROWS), :] = jnp.where(left, x, pltpu.roll(y, 64, 1))
        edge[pl.ds((p + PAIRS) * ROWS, ROWS), :] = jnp.where(left, pltpu.roll(x, 64, 1), y)
    for out, source, at, a, b, c in ((fwd, fwd_in, C_FWD, 7, 6, 5), (bwd, bwd_in, C_BWD, 0, 1, 2)):
        out[pl.ds(0, at), :] = source[...]
        for i in range(3):
            out[pl.ds(at + i * 8, 8), :] = edge[pl.ds(i * 64 + a, 8, stride=8), :]
        out[pl.ds(at + 24, 8), :] = edge[pl.ds(128 + b, 8, stride=8), :]
        out[pl.ds(at + 32, 8), :] = edge[pl.ds(128 + c, 8, stride=8), :]


def kappa_of(wet, below):
    return wet * (0.02 + 0.1 / (1.0 + 10.0 * below * below))


def density(t, s):
    return 0.25 * s - 0.2 * t


def laplace(a, ae, aw, an, as_, we, ww, wn, ws):
    return we * (ae - a) - ww * (a - aw) + wn * (an - a) - ws * (a - as_)


def parts(transport, diffuse):
    return jnp.maximum(transport, 0.0) + diffuse, jnp.minimum(transport, 0.0) - diffuse


def step_weights(te, de, tw, dw, tn, dn, ts, ds):
    ae, be = parts(te, de)
    aw, bw = parts(tw, dw)
    an, bn = parts(tn, dn)
    as_, bs = parts(ts, ds)
    return 1.0 - SUB * (ae - bw + an - bs), -SUB * be, SUB * aw, -SUB * bn, SUB * as_


def react(adv, rate_at, wet, gain, store):
    nutrient = adv[0]
    square = nutrient * nutrient
    uptake = gain * adv[1] * square / (1.0 + square)
    for t in range(NTR):
        total = adv[t]
        for s in range(NTR):
            total = total + rate_at(t, s) * adv[s]
        if t == 0:
            total = total - uptake
        if t == 1:
            total = total + uptake
        store(t, wet * total)


def step(total_rows, vel, thk, hyd, trc, land, bottom, biome, rates, rr, lat_s, lat_n, edge,
         out_vel, out_thk, out_hyd, out_trc, out_abs,
         ex, es, mp, l1s, l1n, lw, c1, cf, half_rate):
    first = (lax.axis_index("lat") * ROWS).astype(F32)

    def latitude(row):
        return 2.0 * (first + row + 0.5) / total_rows - 1.0

    for t in range(NTR):
        for s in range(NTR):
            half_rate[t * NTR + s] = SUB * rr[t, s]

    def rate_at(t, s):
        return half_rate[t * NTR + s]

    lane = lanes((ROWS, COLS))
    sub = subs((ROWS, COLS))
    at_first, at_last = lane == 0, lane == COLS - 1
    top_row, end_row = sub == 0, sub == ROWS - 1

    def mprime(value):
        return jnp.where((lane & 7) == 5, pltpu.roll(value, 2, 1), pltpu.roll(value, 64, 1))

    cor_s = lat_s.at[pl.ds(C_FWD, 40), :]
    cor_n = lat_n.at[pl.ds(C_BWD, 40), :]

    for f in range(NF - 1):
        own = edge[pl.ds(f * ROWS, ROWS), :]
        mp[f] = mprime(own)
        if f >= NTR:
            ex[f, 0:8, :] = jnp.zeros((8, COLS), F32)
            ex[f, 16:24, :] = jnp.zeros((8, COLS), F32)
            for i, at in ((1, 24), (2, 32)):
                ex[f, 7 - i:8 - i, :] = cor_s[at + f - 16:at + f - 15, :]
                ex[f, 16 + i:17 + i, :] = cor_n[at + f - 16:at + f - 15, :]
        ex[f, 7:8, :] = cor_s[f:f + 1, :]
        ex[f, 16:17, :] = cor_n[f:f + 1, :]
        ex[f, 8:16, :] = own

    def east(a):
        return pltpu.roll(a, COLS - 1, 1)

    def west(a):
        return pltpu.roll(a, 1, 1)

    def north(a):
        return pltpu.roll(a, 23, 0)

    def south(a):
        return pltpu.roll(a, 1, 0)

    big = (24, COLS)
    layer = 7 - ((lanes(big) >> 3) & 7)
    u, v, h, t_, s_ = ex[FU], ex[FV], ex[FH], ex[FT], ex[FS]
    wet = (layer.astype(F32) < ex[FD]).astype(F32)
    rho = density(t_, s_)
    p = 0.3 * h + rho
    cor = 0.3 * latitude((subs(big) - 8).astype(F32))
    we = wet * east(wet)
    wn = wet * north(wet)
    ww, ws = west(we), south(wn)
    lap_u = laplace(u, east(u), west(u), north(u), south(u), we, ww, wn, ws)
    lap_v = laplace(v, east(v), west(v), north(v), south(v), we, ww, wn, ws)
    new_u = we * (u + cor * v - (east(p) - p) + 0.1 * lap_u)
    new_v = wn * (v - cor * u - (north(p) - p) + 0.1 * lap_v)
    qe = we * u * 0.5 * (h + east(h))
    qn = wn * v * 0.5 * (h + north(h))
    new_h = wet * (h - (qe - west(qe) + qn - south(qn)))
    kap = kappa_of(wet, jnp.where(layer < K - 1, pltpu.roll(rho, 8, 1) - rho, 0.0))
    te = new_u * 0.5 * (new_h + east(new_h))
    tn = new_v * 0.5 * (new_h + north(new_h))
    de = we * 0.5 * (kap + east(kap))
    dn = wn * 0.5 * (kap + north(kap))
    for i, value in enumerate((new_h, kap, te, de)):
        es[i] = value
        mp[FD + 1 + i] = mprime(value[8:16])
    weights = step_weights(te, de, west(te), west(de), tn, dn, south(tn), south(dn))
    weights = [w[8:16] for w in weights]
    small_layer = 7 - ((lane >> 3) & 7)
    wet8 = wet[8:16]
    chl = ex[1, 8:16, :]
    att = wet8 * (0.1 + 0.2 * chl * chl)
    total = att
    for shift in (1, 2, 4):
        total = total + jnp.where(small_layer >= shift, pltpu.roll(total, COLS - 8 * shift, 1), 0.0)
    lat8 = latitude(sub.astype(F32))
    sun8 = 1.0 - 0.8 * lat8 * lat8
    grow8 = jnp.zeros((ROWS, COLS), F32)
    for r in range(ROWS):
        grow8 = jnp.where(sub == r, growth_of(biome, rates, r), grow8)
    gain = SUB * grow8 * sun8 * jnp.exp(-(total - att))
    adv = []
    for t in range(NTR):
        c = ex[t, 8:16, :]
        w0, w1, w2, w3, w4 = weights
        adv.append(w0 * c + w1 * east(c) + w2 * west(c) + w3 * ex[t, 9:17, :] + w4 * ex[t, 7:15, :])

    def keep_edge(t, value):
        mp[NF + 4 + t] = mprime(value)

    react(adv, rate_at, wet8, gain, keep_edge)

    def layered(row):
        return jnp.broadcast_to(row, (K, COLS))

    def from_west(row):
        return pltpu.roll(layered(row), 69, 1, stride=8, stride_axis=0)

    def from_east(row):
        return pltpu.roll(layered(row), 3, 1, stride=8, stride_axis=0)

    def lat_east(a, row):
        return jnp.where(at_last, from_east(row), east(a))

    def lat_west(a, row):
        return jnp.where(at_first, from_west(row), west(a))

    kf = sub.astype(F32)
    own_depth = depth_of(land, bottom)
    mp_depth = own_depth
    lw[0] = mp_depth

    def block(ref, i):
        return ref[pl.ds(i * K, K), :]

    class Line:
        pass

    def line(ref, misc, base, er, depth_row):
        o = Line()
        o.u, o.v, o.h, o.t, o.s = (block(ref, base + i) for i in range(5))
        o.wet = (kf < layered(ref[misc * K + depth_row:misc * K + depth_row + 1, :])).astype(F32)
        o.er = er
        return around(o)

    def around(o):
        er = o.er
        o.p = 0.3 * o.h + density(o.t, o.s)

        def e(f):
            return ex[f, er:er + 1, :]

        o.ue, o.uw = lat_east(o.u, e(FU)), lat_west(o.u, e(FU))
        o.ve, o.vw = lat_east(o.v, e(FV)), lat_west(o.v, e(FV))
        o.he, o.hw = lat_east(o.h, e(FH)), lat_west(o.h, e(FH))
        pe = 0.3 * e(FH) + density(e(FT), e(FS))
        o.pe = lat_east(o.p, pe)
        wet_e = (kf < from_east(e(FD))).astype(F32)
        wet_w = (kf < from_west(e(FD))).astype(F32)
        o.we = o.wet * jnp.where(at_last, wet_e, east(o.wet))
        o.ww = o.wet * jnp.where(at_first, wet_w, west(o.wet))
        rho = density(o.t, o.s)
        o.kap = kappa_of(o.wet, jnp.where(sub < K - 1, pltpu.roll(rho, K - 1, 0) - rho, 0.0))
        return o

    def own_line(row):
        o = Line()
        o.u, o.v, o.h = layer_rows(vel, 0, row), layer_rows(vel, K, row), layer_rows(thk, 0, row)
        o.p = 0.3 * o.h + density(layer_rows(hyd, 0, row), layer_rows(hyd, K, row))
        o.wet = (kf < layered(lw[0, row:row + 1, :])).astype(F32)
        return o

    def height(o, n, s):
        wn, ws = o.wet * n.wet, o.wet * s.wet
        qe = o.we * o.u * 0.5 * (o.h + o.he)
        qw = o.ww * o.uw * 0.5 * (o.hw + o.h)
        qn = wn * o.v * 0.5 * (o.h + n.h)
        qs = ws * s.v * 0.5 * (s.h + o.h)
        return o.wet * (o.h - (qe - qw + qn - qs))

    def east_speed(o, n, s, cor):
        wn, ws = o.wet * n.wet, o.wet * s.wet
        return o.we * (o.u + cor * o.v - (o.pe - o.p) + 0.1 * laplace(o.u, o.ue, o.uw, n.u, s.u, o.we, o.ww, wn, ws))

    def north_speed(o, n, s, cor):
        wn, ws = o.wet * n.wet, o.wet * s.wet
        return wn * (o.v - cor * o.u - (n.p - o.p) + 0.1 * laplace(o.v, o.ve, o.vw, n.v, s.v, o.we, o.ww, wn, ws))

    sa = line(lat_s, N_FWD - 1, B_DA, 7, 7)
    sb = line(lat_s, N_FWD - 1, B_DB, 6, 6)
    sc = Line()
    sc.v, sc.h = block(lat_s, B_C), block(lat_s, B_C + 1)
    sc.wet = (kf < layered(lat_s[(N_FWD - 1) * K + 5:(N_FWD - 1) * K + 6, :])).astype(F32)
    na = line(lat_n, N_BWD - 1, B_DA, 16, 0)
    nb = line(lat_n, N_BWD - 1, B_DB, 17, 1)
    nc = Line()
    nc.h = block(lat_n, B_C)
    nc.wet = (kf < layered(lat_n[(N_BWD - 1) * K + 2:(N_BWD - 1) * K + 3, :])).astype(F32)
    row0, row7 = own_line(0), own_line(ROWS - 1)

    sa.nu = east_speed(sa, row0, sb, 0.3 * latitude(-1.0))
    sa.nv = north_speed(sa, row0, sb, 0.3 * latitude(-1.0))
    sa.nh = height(sa, row0, sb)
    sb.nv = north_speed(sb, sa, sc, 0.3 * latitude(-2.0))
    sb.nh = height(sb, sa, sc)
    na.nu = east_speed(na, nb, row7, 0.3 * latitude(float(ROWS)))
    na.nv = north_speed(na, nb, row7, 0.3 * latitude(float(ROWS)))
    na.nh = height(na, nb, row7)
    nb.nh = height(nb, nc, na)
    for i, value in enumerate((sa.nv, sa.nh, sa.kap, na.nh, na.kap)):
        lw[1 + i] = value

    lat_col = latitude(sub.astype(F32))
    cor8 = 0.3 * lat_col
    depth_mp = mp[FD]

    def row_of(ref, at):
        return jnp.broadcast_to(ref[pl.ds(at, 1), :], (ROWS, COLS))

    def around_sides(value, f, shift):
        edge_value = pltpu.roll(mp[f], shift, 1)
        return jnp.where(at_last, edge_value, east(value)), jnp.where(at_first, edge_value, west(value))

    def around_ends(value, rn, rs):
        return jnp.where(end_row, rn, pltpu.roll(value, ROWS - 1, 0)), jnp.where(top_row, rs, pltpu.roll(value, 1, 0))

    dep_e, dep_w = around_sides(own_depth, FD, 67)
    dep_n, dep_s = around_ends(own_depth, row_of(lat_n, (N_BWD - 1) * K), row_of(lat_s, (N_FWD - 1) * K + 7))

    def cells(k, over):
        shift = 67 + 8 * k
        kk = k.astype(F32)
        at = pl.ds(pl.multiple_of(k * ROWS, ROWS), ROWS)
        at2 = pl.ds(pl.multiple_of((k + K) * ROWS, ROWS), ROWS)
        u, v, h, t_, s_ = vel[at, :], vel[at2, :], thk[at, :], hyd[at, :], hyd[at2, :]
        wet = (kk < own_depth).astype(F32)
        we = wet * (kk < dep_e).astype(F32)
        ww = wet * (kk < dep_w).astype(F32)
        wn = wet * (kk < dep_n).astype(F32)
        ws = wet * (kk < dep_s).astype(F32)

        def near(value, f, i):
            e, w = around_sides(value, f, shift)
            n, s = around_ends(value, row_of(lat_n, (B_DA + i) * K + k), row_of(lat_s, (B_DA + i) * K + k))
            return e, w, n, s

        ue, uw, un, us = near(u, FU, 0)
        ve, vw, vn, vs = near(v, FV, 1)
        he, hw, hn, hs = near(h, FH, 2)
        t_e, tw, t_n, ts = near(t_, FT, 3)
        s_e, sw, s_n, ss = near(s_, FS, 4)
        p = 0.3 * h + density(t_, s_)
        pe = 0.3 * he + density(t_e, s_e)
        pn = 0.3 * hn + density(t_n, s_n)
        nu = we * (u + cor8 * v - (pe - p) + 0.1 * laplace(u, ue, uw, un, us, we, ww, wn, ws))
        nv = wn * (v - cor8 * u - (pn - p) + 0.1 * laplace(v, ve, vw, vn, vs, we, ww, wn, ws))
        qe = we * u * 0.5 * (h + he)
        qw = ww * uw * 0.5 * (hw + h)
        qn = wn * v * 0.5 * (h + hn)
        qs = ws * vs * 0.5 * (hs + h)
        nh = wet * (h - (qe - qw + qn - qs))
        out_vel[at, :] = nu
        out_vel[at2, :] = nv
        out_thk[at, :] = nh
        lower = jnp.minimum(k + 1, K - 1)
        al = pl.ds(pl.multiple_of(lower * ROWS, ROWS), ROWS)
        al2 = pl.ds(pl.multiple_of((lower + K) * ROWS, ROWS), ROWS)
        below = density(hyd[al, :], hyd[al2, :]) - density(t_, s_)
        kap = kappa_of(wet, below)
        chl = trc[pl.ds(pl.multiple_of((k + K) * ROWS, ROWS), ROWS), :]
        att = wet * (0.1 + 0.2 * chl * chl)
        light = sun8 * jnp.exp(-over)
        absorbed = light * (1.0 - jnp.exp(-att))
        out_abs[at, :] = absorbed
        out_hyd[at, :] = wet * (t_ + 0.1 * laplace(t_, t_e, tw, t_n, ts, we, ww, wn, ws)) + absorbed
        out_hyd[at2, :] = wet * (s_ + 0.1 * laplace(s_, s_e, sw, s_n, ss, we, ww, wn, ws))
        nhe = jnp.where(at_last, pltpu.roll(mp[FD + 1], shift, 1), east(nh))
        kape = jnp.where(at_last, pltpu.roll(mp[FD + 2], shift, 1), east(kap))
        nhn = jnp.where(end_row, row_of(lw.at[4], k), pltpu.roll(nh, ROWS - 1, 0))
        kapn = jnp.where(end_row, row_of(lw.at[5], k), pltpu.roll(kap, ROWS - 1, 0))
        te = nu * 0.5 * (nh + nhe)
        de = we * 0.5 * (kap + kape)
        tn = nv * 0.5 * (nh + nhn)
        dn = wn * 0.5 * (kap + kapn)
        tw = jnp.where(at_first, pltpu.roll(mp[FD + 3], shift, 1), west(te))
        dw = jnp.where(at_first, pltpu.roll(mp[FD + 4], shift, 1), west(de))
        ts = jnp.where(top_row, row_of(lw.at[1], k) * 0.5 * (row_of(lw.at[2], k) + nh), pltpu.roll(tn, 1, 0))
        ds = jnp.where(top_row, ws * 0.5 * (row_of(lw.at[3], k) + kap), pltpu.roll(dn, 1, 0))
        for i, w in enumerate(step_weights(te, de, tw, dw, tn, dn, ts, ds)):
            cf[i, at, :] = w
        cf[5, at, :] = SUB * grow8 * light
        cf[6, at, :] = tn
        cf[7, at, :] = dn
        return over + att

    lax.fori_loop(0, K, cells, jnp.zeros((ROWS, COLS), F32))

    def outer(o, te_row, grow, lat_row, tn, dn, ts, ds, near_ref, north_of, south_of, er, kept):
        he = lat_east(o.nh, es[0, er:er + 1, :])
        kape = lat_east(o.kap, es[1, er:er + 1, :])
        te = o.nu * 0.5 * (o.nh + he)
        de = o.we * 0.5 * (o.kap + kape)
        tw = lat_west(te, es[2, er:er + 1, :])
        dw = lat_west(de, es[3, er:er + 1, :])
        w0, w1, w2, w3, w4 = step_weights(te, de, tw, dw, tn, dn, ts, ds)
        chl = block(near_ref, B_A + 1)
        att = o.wet * (0.1 + 0.2 * chl * chl)
        total = att
        for shift in (1, 2, 4):
            total = total + jnp.where(sub >= shift, pltpu.roll(total, shift, 0), 0.0)
        lat_here = latitude(lat_row)
        gain = SUB * layered(grow) * ((1.0 - 0.8 * lat_here * lat_here) * jnp.exp(-(total - att)))
        adv = []
        for t in range(NTR):
            c = block(near_ref, B_A + t)
            row = ex[t, er:er + 1, :]
            adv.append(w0 * c + w1 * lat_east(c, row) + w2 * lat_west(c, row) + w3 * north_of(t) + w4 * south_of(t))

        def keep(t, value):
            kept[pl.ds(t * K, K), :] = value

        react(adv, rate_at, o.wet, gain, keep)

    h0 = layer_rows(out_thk, 0, 0)
    kap0 = kappa_of(row0.wet, row_below(hyd, 0, sub))
    wn_s = sa.wet * row0.wet
    outer(sa, None, lat_s[(N_FWD - 1) * K + 3:(N_FWD - 1) * K + 4, :], -1.0,
          sa.nv * 0.5 * (sa.nh + h0), wn_s * 0.5 * (sa.kap + kap0),
          sb.nv * 0.5 * (sb.nh + sa.nh), sb.wet * sa.wet * 0.5 * (sb.kap + sa.kap),
          lat_s, lambda t: layer_rows(trc, t * K, 0), lambda t: block(lat_s, B_B + t), 7, l1s)
    outer(na, None, lat_n[(N_BWD - 1) * K + 3:(N_BWD - 1) * K + 4, :], float(ROWS),
          na.nv * 0.5 * (na.nh + nb.nh), na.wet * nb.wet * 0.5 * (na.kap + nb.kap),
          layer_rows(cf.at[6], 0, ROWS - 1), layer_rows(cf.at[7], 0, ROWS - 1),
          lat_n, lambda t: block(lat_n, B_B + t), lambda t: layer_rows(trc, t * K, ROWS - 1), 16, l1n)

    def substep(src, dst, mp_base, end_n, end_s):
        def body(k, carry):
            shift = 67 + 8 * k
            at = pl.ds(pl.multiple_of(k * ROWS, ROWS), ROWS)
            w0, w1, w2, w3, w4 = (cf[i, at, :] for i in range(5))
            wet = (k.astype(F32) < own_depth).astype(F32)
            adv = []
            for t in range(NTR):
                c = src[pl.ds(pl.multiple_of((t * K + k) * ROWS, ROWS), ROWS), :]
                e, w = around_sides(c, mp_base + t, shift)
                n, s = around_ends(c, row_of(end_n, t * K + k), row_of(end_s, t * K + k))
                adv.append(w0 * c + w1 * e + w2 * w + w3 * n + w4 * s)

            def keep(t, value):
                dst[pl.ds(pl.multiple_of((t * K + k) * ROWS, ROWS), ROWS), :] = value

            react(adv, rate_at, wet, cf[5, at, :], keep)
            return carry

        lax.fori_loop(0, K, body, 0)

    substep(trc, c1, 0, lat_n, lat_s)
    substep(c1, out_trc, NF + 4, l1n, l1s)


def row_below(hyd, row, sub):
    rho = density(layer_rows(hyd, 0, row), layer_rows(hyd, K, row))
    return jnp.where(sub < K - 1, pltpu.roll(rho, K - 1, 0) - rho, 0.0)


def near(*dims):
    return pltpu.VMEM(dims, F32)


def far(*dims):
    return jax.ShapeDtypeStruct(dims, F32)


def held(x):
    return pltpu.with_memory_space_constraint(x, pltpu.VMEM)


def call(kernel, out_shape, spaces, scratch=(), flops=100000):
    spec = {"v": pl.BlockSpec(memory_space=pltpu.VMEM), "s": pl.BlockSpec(memory_space=pltpu.SMEM)}
    return pl.pallas_call(
        kernel,
        out_shape=out_shape,
        in_specs=[spec[c] for c in spaces],
        out_specs=tuple(spec["v"] for _ in out_shape),
        scratch_shapes=list(scratch),
        cost_estimate=pl.CostEstimate(flops=flops, bytes_accessed=100000, transcendentals=0),
    )


def per_device(velocity, thickness, hydrography, tracers, land_mask, bottom_layer, row_biome, reaction_rates, growth_rates):
    lat, lon = lax.axis_size("lat"), lax.axis_size("lon")
    vel = velocity.reshape(2 * K * ROWS, COLS)
    thk = thickness.reshape(K * ROWS, COLS)
    hyd = hydrography.reshape(2 * K * ROWS, COLS)
    trc = tracers.reshape(NTR * K * ROWS, COLS)
    state = (vel, thk, hyd, trc, land_mask, bottom_layer)

    def swap(n, start):
        return [p for i in range(start, n - 1, 2) for p in ((i, i + 1), (i + 1, i))]

    (own,) = call(lon_pack, (near(PAIRS * ROWS, COLS),), "vvvvvv")(*state)
    own = held(own)
    outer = held(lax.ppermute(own, "lon", swap(lon, 1)))
    inner = held(lax.ppermute(own, "lon", swap(lon, 0)))
    fwd, bwd = call(lat_pack, (near(C_FWD, COLS), near(C_BWD, COLS)), "vvvvvvvss")(
        *state, own, row_biome, growth_rates)
    edge, fwd, bwd = call(
        edge_pack, (near(NF * ROWS, COLS), near(ROWS_FWD, COLS), near(ROWS_BWD, COLS)), "vvvvv"
    )(own, inner, outer, held(fwd), held(bwd))
    lat_s = held(lax.ppermute(fwd, "lat", [(i, i + 1) for i in range(lat - 1)]))
    lat_n = held(lax.ppermute(bwd, "lat", [(i + 1, i) for i in range(lat - 1)]))

    def body(*refs):
        step(lat * ROWS, *refs)

    outs = call(
        body,
        (far(2 * K * ROWS, COLS), far(K * ROWS, COLS), far(2 * K * ROWS, COLS), far(NTR * K * ROWS, COLS), far(K * ROWS, COLS)),
        "vvvvvvsssvvv",
        scratch=[
            pltpu.VMEM((NF, 24, COLS), F32),
            pltpu.VMEM((4, 24, COLS), F32),
            pltpu.VMEM((NF + 4 + NTR, ROWS, COLS), F32),
            pltpu.VMEM((NTR * K, COLS), F32),
            pltpu.VMEM((NTR * K, COLS), F32),
            pltpu.VMEM((6, ROWS, COLS), F32),
            pltpu.VMEM((NTR * K * ROWS, COLS), F32),
            pltpu.VMEM((8, K * ROWS, COLS), F32),
            pltpu.SMEM((NTR * NTR,), F32),
        ],
    )(*state, row_biome, growth_rates, reaction_rates, lat_s, lat_n, held(edge))
    new_vel, new_thk, new_hyd, new_trc, absorbed = outs
    return (new_vel.reshape(velocity.shape), new_thk.reshape(thickness.shape), new_hyd.reshape(hydrography.shape),
            new_trc.reshape(tracers.shape), absorbed.reshape(thickness.shape))


def solution(mesh):
    field = P(None, "lat", "lon")
    fields = P(None, None, "lat", "lon")
    in_specs = (fields, field, fields, fields, P("lat", "lon"), P("lat", "lon"), P("lat"), P(), P())
    out_specs = (fields, field, fields, fields, field)
    return jax.shard_map(per_device, mesh=mesh, in_specs=in_specs, out_specs=out_specs, check_vma=False)
```

```python
import jax
import jax.numpy as jnp
from jax import lax
from jax.experimental import pallas as pl
from jax.experimental.pallas import tpu as pltpu
from jax.sharding import PartitionSpec as P

F32 = jnp.float32
NSUB = 2
SUB = 1.0 / NSUB
NTR = 17
K = 8
ROWS = 8
COLS = 128
FU, FV, FH, FT, FS, FD = 17, 18, 19, 20, 21, 22
NF = 24
PAIRS = NF // 2
B_A, B_B, B_DA, B_DB, B_C = 0, 17, 34, 39, 44
N_FWD, N_BWD = 47, 46
C_FWD, C_BWD = N_FWD * K, N_BWD * K
ROWS_FWD, ROWS_BWD = C_FWD + 40, C_BWD + 40


def lanes(shape):
    return lax.broadcasted_iota(jnp.int32, shape, len(shape) - 1)


def subs(shape):
    return lax.broadcasted_iota(jnp.int32, shape, len(shape) - 2)


def growth_of(biome_ref, rates_ref, row):
    kind = biome_ref[row]
    rate = rates_ref[0]
    for i in range(1, rates_ref.shape[0]):
        rate = jnp.where(kind == i, rates_ref[i], rate)
    return rate


def layer_rows(ref, plane, row):
    return ref[pl.ds(plane * ROWS + row, K, stride=ROWS), :]


def lat_pack(vel, thk, hyd, trc, depth_ref, after, biome, rates, fwd, bwd):
    depth = depth_ref[...]
    sub = subs((ROWS, COLS))

    def put(out, block, value):
        out[pl.ds(block * K, K), :] = value

    def state(out, block, row):
        put(out, block, layer_rows(vel, 0, row))
        put(out, block + 1, layer_rows(vel, K, row))
        put(out, block + 2, layer_rows(thk, 0, row))
        put(out, block + 3, layer_rows(hyd, 0, row))
        put(out, block + 4, layer_rows(hyd, K, row))

    for out, a, b in ((fwd, ROWS - 1, ROWS - 2), (bwd, 0, 1)):
        for t in range(NTR):
            put(out, B_A + t, layer_rows(trc, t * K, a))
            put(out, B_B + t, layer_rows(trc, t * K, b))
        state(out, B_DA, a)
        state(out, B_DB, b)
    put(fwd, B_C, layer_rows(vel, K, ROWS - 3))
    put(fwd, B_C + 1, layer_rows(thk, 0, ROWS - 3))
    put(bwd, B_C, layer_rows(thk, 0, 2))
    put(fwd, N_FWD - 1, jnp.where(sub == 3, growth_of(biome, rates, ROWS - 1), depth))
    put(bwd, N_BWD - 1, jnp.where(sub == 3, growth_of(biome, rates, 0), depth))


def lon_pack(vel_in, thk_in, hyd_in, trc_in, land, bottom, vel, thk, hyd, trc, depth_out, out, sems):
    moves = [
        pltpu.make_async_copy(src, dst, sems.at[i])
        for i, (src, dst) in enumerate(((trc_in, trc), (vel_in, vel), (hyd_in, hyd), (thk_in, thk)))
    ]
    for move in moves:
        move.start()
    depth = (land[...] * bottom[...]).astype(F32)
    depth_out[...] = depth
    for move in moves[::-1]:
        move.wait()
    group = lanes((ROWS, COLS)) >> 3

    def plane(f, k):
        if f < NTR:
            return trc[pl.ds((f * K + k) * ROWS, ROWS), :]
        if f < FH:
            return vel[pl.ds(((f - FU) * K + k) * ROWS, ROWS), :]
        if f == FH:
            return thk[pl.ds(k * ROWS, ROWS), :]
        if f < FD:
            return hyd[pl.ds(((f - FT) * K + k) * ROWS, ROWS), :]
        return depth

    for p in range(PAIRS):
        packed = jnp.zeros((ROWS, COLS), F32)
        for half in range(2):
            f = p + PAIRS * half
            if f > FD:
                continue
            for k in range(K):
                moved = pltpu.roll(plane(f, k), (half * 64 + (7 - k) * 8 + 4) % COLS, 1)
                packed = jnp.where(group == half * 8 + 7 - k, moved, packed)
        out[pl.ds(p * ROWS, ROWS), :] = packed


def edge_pack(own, inner, outer, fwd_in, bwd_in, edge, fwd, bwd):
    lane = lanes((ROWS, COLS))
    low = (lane & 7) < 4
    left = lane < 64
    odd = jnp.full((ROWS, COLS), lax.axis_index("lon") & 1) == 1
    for p in range(PAIRS):
        at = pl.ds(p * ROWS, ROWS)
        o, a, b = own[at, :], inner[at, :], outer[at, :]
        x = jnp.where(low, jnp.where(odd, a, b), o)
        y = jnp.where(low, o, jnp.where(odd, b, a))
        edge[pl.ds(p * ROWS, ROWS), :] = jnp.where(left, x, pltpu.roll(y, 64, 1))
        edge[pl.ds((p + PAIRS) * ROWS, ROWS), :] = jnp.where(left, pltpu.roll(x, 64, 1), y)
    for out, source, at, a, b, c in ((fwd, fwd_in, C_FWD, 7, 6, 5), (bwd, bwd_in, C_BWD, 0, 1, 2)):
        out[pl.ds(0, at), :] = source[...]
        for i in range(3):
            out[pl.ds(at + i * 8, 8), :] = edge[pl.ds(i * 64 + a, 8, stride=8), :]
        out[pl.ds(at + 24, 8), :] = edge[pl.ds(128 + b, 8, stride=8), :]
        out[pl.ds(at + 32, 8), :] = edge[pl.ds(128 + c, 8, stride=8), :]


def kappa_of(wet, below):
    return wet * (0.02 + 0.1 / (1.0 + 10.0 * below * below))


def density(t, s):
    return 0.25 * s - 0.2 * t


def laplace(a, ae, aw, an, as_, we, ww, wn, ws):
    return we * (ae - a) - ww * (a - aw) + wn * (an - a) - ws * (a - as_)


def parts(transport, diffuse):
    return jnp.maximum(transport, 0.0) + diffuse, jnp.minimum(transport, 0.0) - diffuse


def step_weights(te, de, tw, dw, tn, dn, ts, ds):
    ae, be = parts(te, de)
    aw, bw = parts(tw, dw)
    an, bn = parts(tn, dn)
    as_, bs = parts(ts, ds)
    return 1.0 - SUB * (ae - bw + an - bs), -SUB * be, SUB * aw, -SUB * bn, SUB * as_


def react(adv, rate_at, wet, gain, store):
    nutrient = adv[0]
    square = nutrient * nutrient
    uptake = gain * adv[1] * square / (1.0 + square)
    for t in range(NTR):
        total = adv[t]
        for s in range(NTR):
            total = total + rate_at(t, s) * adv[s]
        if t == 0:
            total = total - uptake
        if t == 1:
            total = total + uptake
        store(t, wet * total)


def step(total_rows, vel, thk, hyd, trc, depth_ref, biome, rates, table, lat_s, lat_n, edge,
         out_vel, out_thk, out_hyd, out_trc, out_abs,
         ex, es, mp, l1s, l1n, lw, c1, cf):
    first = (lax.axis_index("lat") * ROWS).astype(F32)

    def latitude(row):
        return 2.0 * (first + row + 0.5) / total_rows - 1.0

    def rate_at(t, s):
        return table[pl.ds((t * NTR + s) * ROWS, ROWS), :]

    lane = lanes((ROWS, COLS))
    sub = subs((ROWS, COLS))
    at_first, at_last = lane == 0, lane == COLS - 1
    top_row, end_row = sub == 0, sub == ROWS - 1

    def mprime(value):
        return jnp.where((lane & 7) == 5, pltpu.roll(value, 2, 1), pltpu.roll(value, 64, 1))

    cor_s = lat_s.at[pl.ds(C_FWD, 40), :]
    cor_n = lat_n.at[pl.ds(C_BWD, 40), :]

    for f in range(NF - 1):
        own = edge[pl.ds(f * ROWS, ROWS), :]
        mp[f] = mprime(own)
        if f >= NTR:
            ex[f, 0:8, :] = jnp.zeros((8, COLS), F32)
            ex[f, 16:24, :] = jnp.zeros((8, COLS), F32)
            for i, at in ((1, 24), (2, 32)):
                ex[f, 7 - i:8 - i, :] = cor_s[at + f - 16:at + f - 15, :]
                ex[f, 16 + i:17 + i, :] = cor_n[at + f - 16:at + f - 15, :]
        ex[f, 7:8, :] = cor_s[f:f + 1, :]
        ex[f, 16:17, :] = cor_n[f:f + 1, :]
        ex[f, 8:16, :] = own

    def east(a):
        return pltpu.roll(a, COLS - 1, 1)

    def west(a):
        return pltpu.roll(a, 1, 1)

    def north(a):
        return pltpu.roll(a, 23, 0)

    def south(a):
        return pltpu.roll(a, 1, 0)

    big = (24, COLS)
    layer = 7 - ((lanes(big) >> 3) & 7)
    u, v, h, t_, s_ = ex[FU], ex[FV], ex[FH], ex[FT], ex[FS]
    wet = (layer.astype(F32) < ex[FD]).astype(F32)
    rho = density(t_, s_)
    p = 0.3 * h + rho
    cor = 0.3 * latitude((subs(big) - 8).astype(F32))
    we = wet * east(wet)
    wn = wet * north(wet)
    ww, ws = west(we), south(wn)
    lap_u = laplace(u, east(u), west(u), north(u), south(u), we, ww, wn, ws)
    lap_v = laplace(v, east(v), west(v), north(v), south(v), we, ww, wn, ws)
    new_u = we * (u + cor * v - (east(p) - p) + 0.1 * lap_u)
    new_v = wn * (v - cor * u - (north(p) - p) + 0.1 * lap_v)
    qe = we * u * 0.5 * (h + east(h))
    qn = wn * v * 0.5 * (h + north(h))
    new_h = wet * (h - (qe - west(qe) + qn - south(qn)))
    kap = kappa_of(wet, jnp.where(layer < K - 1, pltpu.roll(rho, 8, 1) - rho, 0.0))
    te = new_u * 0.5 * (new_h + east(new_h))
    tn = new_v * 0.5 * (new_h + north(new_h))
    de = we * 0.5 * (kap + east(kap))
    dn = wn * 0.5 * (kap + north(kap))
    for i, value in enumerate((new_h, kap, te, de)):
        es[i] = value
        mp[FD + 1 + i] = mprime(value[8:16])
    weights = step_weights(te, de, west(te), west(de), tn, dn, south(tn), south(dn))
    weights = [w[8:16] for w in weights]
    small_layer = 7 - ((lane >> 3) & 7)
    wet8 = wet[8:16]
    chl = ex[1, 8:16, :]
    att = wet8 * (0.1 + 0.2 * chl * chl)
    total = att
    for shift in (1, 2, 4):
        total = total + jnp.where(small_layer >= shift, pltpu.roll(total, COLS - 8 * shift, 1), 0.0)
    lat8 = latitude(sub.astype(F32))
    sun8 = 1.0 - 0.8 * lat8 * lat8
    grow8 = jnp.zeros((ROWS, COLS), F32)
    for r in range(ROWS):
        grow8 = jnp.where(sub == r, growth_of(biome, rates, r), grow8)
    gain = SUB * grow8 * sun8 * jnp.exp(-(total - att))
    adv = []
    for t in range(NTR):
        c = ex[t, 8:16, :]
        w0, w1, w2, w3, w4 = weights
        adv.append(w0 * c + w1 * east(c) + w2 * west(c) + w3 * ex[t, 9:17, :] + w4 * ex[t, 7:15, :])

    def keep_edge(t, value):
        mp[NF + 4 + t] = mprime(value)

    react(adv, rate_at, wet8, gain, keep_edge)

    def layered(row):
        return jnp.broadcast_to(row, (K, COLS))

    def from_west(row):
        return pltpu.roll(layered(row), 69, 1, stride=8, stride_axis=0)

    def from_east(row):
        return pltpu.roll(layered(row), 3, 1, stride=8, stride_axis=0)

    def lat_east(a, row):
        return jnp.where(at_last, from_east(row), east(a))

    def lat_west(a, row):
        return jnp.where(at_first, from_west(row), west(a))

    kf = sub.astype(F32)
    own_depth = depth_ref[...]

    def block(ref, i):
        return ref[pl.ds(i * K, K), :]

    class Line:
        pass

    def line(ref, misc, base, er, depth_row):
        o = Line()
        o.u, o.v, o.h, o.t, o.s = (block(ref, base + i) for i in range(5))
        o.wet = (kf < layered(ref[misc * K + depth_row:misc * K + depth_row + 1, :])).astype(F32)
        o.er = er
        return around(o)

    def around(o):
        er = o.er
        o.p = 0.3 * o.h + density(o.t, o.s)

        def e(f):
            return ex[f, er:er + 1, :]

        o.ue, o.uw = lat_east(o.u, e(FU)), lat_west(o.u, e(FU))
        o.ve, o.vw = lat_east(o.v, e(FV)), lat_west(o.v, e(FV))
        o.he, o.hw = lat_east(o.h, e(FH)), lat_west(o.h, e(FH))
        pe = 0.3 * e(FH) + density(e(FT), e(FS))
        o.pe = lat_east(o.p, pe)
        wet_e = (kf < from_east(e(FD))).astype(F32)
        wet_w = (kf < from_west(e(FD))).astype(F32)
        o.we = o.wet * jnp.where(at_last, wet_e, east(o.wet))
        o.ww = o.wet * jnp.where(at_first, wet_w, west(o.wet))
        rho = density(o.t, o.s)
        o.kap = kappa_of(o.wet, jnp.where(sub < K - 1, pltpu.roll(rho, K - 1, 0) - rho, 0.0))
        return o

    def own_line(row):
        o = Line()
        o.u, o.v, o.h = layer_rows(vel, 0, row), layer_rows(vel, K, row), layer_rows(thk, 0, row)
        o.p = 0.3 * o.h + density(layer_rows(hyd, 0, row), layer_rows(hyd, K, row))
        o.wet = (kf < layered(depth_ref[row:row + 1, :])).astype(F32)
        return o

    def height(o, n, s):
        wn, ws = o.wet * n.wet, o.wet * s.wet
        qe = o.we * o.u * 0.5 * (o.h + o.he)
        qw = o.ww * o.uw * 0.5 * (o.hw + o.h)
        qn = wn * o.v * 0.5 * (o.h + n.h)
        qs = ws * s.v * 0.5 * (s.h + o.h)
        return o.wet * (o.h - (qe - qw + qn - qs))

    def east_speed(o, n, s, cor):
        wn, ws = o.wet * n.wet, o.wet * s.wet
        return o.we * (o.u + cor * o.v - (o.pe - o.p) + 0.1 * laplace(o.u, o.ue, o.uw, n.u, s.u, o.we, o.ww, wn, ws))

    def north_speed(o, n, s, cor):
        wn, ws = o.wet * n.wet, o.wet * s.wet
        return wn * (o.v - cor * o.u - (n.p - o.p) + 0.1 * laplace(o.v, o.ve, o.vw, n.v, s.v, o.we, o.ww, wn, ws))

    sa = line(lat_s, N_FWD - 1, B_DA, 7, 7)
    sb = line(lat_s, N_FWD - 1, B_DB, 6, 6)
    sc = Line()
    sc.v, sc.h = block(lat_s, B_C), block(lat_s, B_C + 1)
    sc.wet = (kf < layered(lat_s[(N_FWD - 1) * K + 5:(N_FWD - 1) * K + 6, :])).astype(F32)
    na = line(lat_n, N_BWD - 1, B_DA, 16, 0)
    nb = line(lat_n, N_BWD - 1, B_DB, 17, 1)
    nc = Line()
    nc.h = block(lat_n, B_C)
    nc.wet = (kf < layered(lat_n[(N_BWD - 1) * K + 2:(N_BWD - 1) * K + 3, :])).astype(F32)
    row0, row7 = own_line(0), own_line(ROWS - 1)

    sa.nu = east_speed(sa, row0, sb, 0.3 * latitude(-1.0))
    sa.nv = north_speed(sa, row0, sb, 0.3 * latitude(-1.0))
    sa.nh = height(sa, row0, sb)
    sb.nv = north_speed(sb, sa, sc, 0.3 * latitude(-2.0))
    sb.nh = height(sb, sa, sc)
    na.nu = east_speed(na, nb, row7, 0.3 * latitude(float(ROWS)))
    na.nv = north_speed(na, nb, row7, 0.3 * latitude(float(ROWS)))
    na.nh = height(na, nb, row7)
    nb.nh = height(nb, nc, na)
    for i, value in enumerate((sa.nv, sa.nh, sa.kap, na.nh, na.kap)):
        lw[1 + i] = value

    lat_col = latitude(sub.astype(F32))
    cor8 = 0.3 * lat_col
    depth_mp = mp[FD]

    def row_of(ref, at):
        return jnp.broadcast_to(ref[pl.ds(at, 1), :], (ROWS, COLS))

    def around_sides(value, f, shift):
        edge_value = pltpu.roll(mp[f], shift, 1)
        return jnp.where(at_last, edge_value, east(value)), jnp.where(at_first, edge_value, west(value))

    def around_ends(value, rn, rs):
        return jnp.where(end_row, rn, pltpu.roll(value, ROWS - 1, 0)), jnp.where(top_row, rs, pltpu.roll(value, 1, 0))

    dep_e, dep_w = around_sides(own_depth, FD, 67)
    dep_n, dep_s = around_ends(own_depth, row_of(lat_n, (N_BWD - 1) * K), row_of(lat_s, (N_FWD - 1) * K + 7))

    def cells(k, over):
        shift = 67 + 8 * k
        kk = k.astype(F32)
        at = pl.ds(pl.multiple_of(k * ROWS, ROWS), ROWS)
        at2 = pl.ds(pl.multiple_of((k + K) * ROWS, ROWS), ROWS)
        u, v, h, t_, s_ = vel[at, :], vel[at2, :], thk[at, :], hyd[at, :], hyd[at2, :]
        wet = (kk < own_depth).astype(F32)
        we = wet * (kk < dep_e).astype(F32)
        ww = wet * (kk < dep_w).astype(F32)
        wn = wet * (kk < dep_n).astype(F32)
        ws = wet * (kk < dep_s).astype(F32)

        def near(value, f, i):
            e, w = around_sides(value, f, shift)
            n, s = around_ends(value, row_of(lat_n, (B_DA + i) * K + k), row_of(lat_s, (B_DA + i) * K + k))
            return e, w, n, s

        ue, uw, un, us = near(u, FU, 0)
        ve, vw, vn, vs = near(v, FV, 1)
        he, hw, hn, hs = near(h, FH, 2)
        t_e, tw, t_n, ts = near(t_, FT, 3)
        s_e, sw, s_n, ss = near(s_, FS, 4)
        p = 0.3 * h + density(t_, s_)
        pe = 0.3 * he + density(t_e, s_e)
        pn = 0.3 * hn + density(t_n, s_n)
        nu = we * (u + cor8 * v - (pe - p) + 0.1 * laplace(u, ue, uw, un, us, we, ww, wn, ws))
        nv = wn * (v - cor8 * u - (pn - p) + 0.1 * laplace(v, ve, vw, vn, vs, we, ww, wn, ws))
        qe = we * u * 0.5 * (h + he)
        qw = ww * uw * 0.5 * (hw + h)
        qn = wn * v * 0.5 * (h + hn)
        qs = ws * vs * 0.5 * (hs + h)
        nh = wet * (h - (qe - qw + qn - qs))
        out_vel[at, :] = nu
        out_vel[at2, :] = nv
        out_thk[at, :] = nh
        lower = jnp.minimum(k + 1, K - 1)
        al = pl.ds(pl.multiple_of(lower * ROWS, ROWS), ROWS)
        al2 = pl.ds(pl.multiple_of((lower + K) * ROWS, ROWS), ROWS)
        below = density(hyd[al, :], hyd[al2, :]) - density(t_, s_)
        kap = kappa_of(wet, below)
        chl = trc[pl.ds(pl.multiple_of((k + K) * ROWS, ROWS), ROWS), :]
        att = wet * (0.1 + 0.2 * chl * chl)
        light = sun8 * jnp.exp(-over)
        absorbed = light * (1.0 - jnp.exp(-att))
        out_abs[at, :] = absorbed
        out_hyd[at, :] = wet * (t_ + 0.1 * laplace(t_, t_e, tw, t_n, ts, we, ww, wn, ws)) + absorbed
        out_hyd[at2, :] = wet * (s_ + 0.1 * laplace(s_, s_e, sw, s_n, ss, we, ww, wn, ws))
        nhe = jnp.where(at_last, pltpu.roll(mp[FD + 1], shift, 1), east(nh))
        kape = jnp.where(at_last, pltpu.roll(mp[FD + 2], shift, 1), east(kap))
        nhn = jnp.where(end_row, row_of(lw.at[4], k), pltpu.roll(nh, ROWS - 1, 0))
        kapn = jnp.where(end_row, row_of(lw.at[5], k), pltpu.roll(kap, ROWS - 1, 0))
        te = nu * 0.5 * (nh + nhe)
        de = we * 0.5 * (kap + kape)
        tn = nv * 0.5 * (nh + nhn)
        dn = wn * 0.5 * (kap + kapn)
        tw = jnp.where(at_first, pltpu.roll(mp[FD + 3], shift, 1), west(te))
        dw = jnp.where(at_first, pltpu.roll(mp[FD + 4], shift, 1), west(de))
        ts = jnp.where(top_row, row_of(lw.at[1], k) * 0.5 * (row_of(lw.at[2], k) + nh), pltpu.roll(tn, 1, 0))
        ds = jnp.where(top_row, ws * 0.5 * (row_of(lw.at[3], k) + kap), pltpu.roll(dn, 1, 0))
        for i, w in enumerate(step_weights(te, de, tw, dw, tn, dn, ts, ds)):
            cf[i, at, :] = w
        cf[5, at, :] = SUB * grow8 * light
        cf[6, at, :] = tn
        cf[7, at, :] = dn
        return over + att

    lax.fori_loop(0, K, cells, jnp.zeros((ROWS, COLS), F32))

    def outer(o, te_row, grow, lat_row, tn, dn, ts, ds, near_ref, north_of, south_of, er, kept):
        he = lat_east(o.nh, es[0, er:er + 1, :])
        kape = lat_east(o.kap, es[1, er:er + 1, :])
        te = o.nu * 0.5 * (o.nh + he)
        de = o.we * 0.5 * (o.kap + kape)
        tw = lat_west(te, es[2, er:er + 1, :])
        dw = lat_west(de, es[3, er:er + 1, :])
        w0, w1, w2, w3, w4 = step_weights(te, de, tw, dw, tn, dn, ts, ds)
        chl = block(near_ref, B_A + 1)
        att = o.wet * (0.1 + 0.2 * chl * chl)
        total = att
        for shift in (1, 2, 4):
            total = total + jnp.where(sub >= shift, pltpu.roll(total, shift, 0), 0.0)
        lat_here = latitude(lat_row)
        gain = SUB * layered(grow) * ((1.0 - 0.8 * lat_here * lat_here) * jnp.exp(-(total - att)))
        adv = []
        for t in range(NTR):
            c = block(near_ref, B_A + t)
            row = ex[t, er:er + 1, :]
            adv.append(w0 * c + w1 * lat_east(c, row) + w2 * lat_west(c, row) + w3 * north_of(t) + w4 * south_of(t))

        def keep(t, value):
            kept[pl.ds(t * K, K), :] = value

        react(adv, rate_at, o.wet, gain, keep)

    h0 = layer_rows(out_thk, 0, 0)
    kap0 = kappa_of(row0.wet, row_below(hyd, 0, sub))
    wn_s = sa.wet * row0.wet
    outer(sa, None, lat_s[(N_FWD - 1) * K + 3:(N_FWD - 1) * K + 4, :], -1.0,
          sa.nv * 0.5 * (sa.nh + h0), wn_s * 0.5 * (sa.kap + kap0),
          sb.nv * 0.5 * (sb.nh + sa.nh), sb.wet * sa.wet * 0.5 * (sb.kap + sa.kap),
          lat_s, lambda t: layer_rows(trc, t * K, 0), lambda t: block(lat_s, B_B + t), 7, l1s)
    outer(na, None, lat_n[(N_BWD - 1) * K + 3:(N_BWD - 1) * K + 4, :], float(ROWS),
          na.nv * 0.5 * (na.nh + nb.nh), na.wet * nb.wet * 0.5 * (na.kap + nb.kap),
          layer_rows(cf.at[6], 0, ROWS - 1), layer_rows(cf.at[7], 0, ROWS - 1),
          lat_n, lambda t: block(lat_n, B_B + t), lambda t: layer_rows(trc, t * K, ROWS - 1), 16, l1n)

    def substep(src, dst, mp_base, end_n, end_s):
        def body(k, carry):
            shift = 67 + 8 * k
            at = pl.ds(pl.multiple_of(k * ROWS, ROWS), ROWS)
            w0, w1, w2, w3, w4 = (cf[i, at, :] for i in range(5))
            wet = (k.astype(F32) < own_depth).astype(F32)
            adv = []
            for t in range(NTR):
                c = src[pl.ds(pl.multiple_of((t * K + k) * ROWS, ROWS), ROWS), :]
                e, w = around_sides(c, mp_base + t, shift)
                n, s = around_ends(c, row_of(end_n, t * K + k), row_of(end_s, t * K + k))
                adv.append(w0 * c + w1 * e + w2 * w + w3 * n + w4 * s)

            def keep(t, value):
                dst[pl.ds(pl.multiple_of((t * K + k) * ROWS, ROWS), ROWS), :] = value

            react(adv, rate_at, wet, cf[5, at, :], keep)
            return carry

        lax.fori_loop(0, K, body, 0)

    substep(trc, c1, 0, lat_n, lat_s)
    substep(c1, out_trc, NF + 4, l1n, l1s)


def row_below(hyd, row, sub):
    rho = density(layer_rows(hyd, 0, row), layer_rows(hyd, K, row))
    return jnp.where(sub < K - 1, pltpu.roll(rho, K - 1, 0) - rho, 0.0)


def rate_table(after, rr, out):
    for t in range(NTR):
        for s in range(NTR):
            out[pl.ds((t * NTR + s) * ROWS, ROWS), :] = jnp.full((ROWS, COLS), SUB * rr[t, s])


def near(*dims):
    return pltpu.VMEM(dims, F32)


def far(*dims):
    return jax.ShapeDtypeStruct(dims, F32)


def held(x):
    return pltpu.with_memory_space_constraint(x, pltpu.VMEM)


def call(kernel, out_shape, spaces, scratch=(), flops=100000):
    spec = {"a": pl.BlockSpec(memory_space=pl.ANY), "v": pl.BlockSpec(memory_space=pltpu.VMEM), "s": pl.BlockSpec(memory_space=pltpu.SMEM)}
    return pl.pallas_call(
        kernel,
        out_shape=out_shape,
        in_specs=[spec[c] for c in spaces],
        out_specs=tuple(spec["v"] for _ in out_shape),
        scratch_shapes=list(scratch),
        cost_estimate=pl.CostEstimate(flops=flops, bytes_accessed=100000, transcendentals=0),
    )


def per_device(velocity, thickness, hydrography, tracers, land_mask, bottom_layer, row_biome, reaction_rates, growth_rates):
    lat, lon = lax.axis_size("lat"), lax.axis_size("lon")
    vel = velocity.reshape(2 * K * ROWS, COLS)
    thk = thickness.reshape(K * ROWS, COLS)
    hyd = hydrography.reshape(2 * K * ROWS, COLS)
    trc = tracers.reshape(NTR * K * ROWS, COLS)

    def swap(n, start):
        return [p for i in range(start, n - 1, 2) for p in ((i, i + 1), (i + 1, i))]

    *state, own = (held(x) for x in call(
        lon_pack,
        (near(2 * K * ROWS, COLS), near(K * ROWS, COLS), near(2 * K * ROWS, COLS), near(NTR * K * ROWS, COLS),
         near(ROWS, COLS), near(PAIRS * ROWS, COLS)),
        "aaaavv",
        scratch=[pltpu.SemaphoreType.DMA((4,))],
    )(vel, thk, hyd, trc, land_mask, bottom_layer))
    outer = held(lax.ppermute(own, "lon", swap(lon, 1)))
    inner = held(lax.ppermute(own, "lon", swap(lon, 0)))
    fwd, bwd = call(lat_pack, (near(C_FWD, COLS), near(C_BWD, COLS)), "vvvvvvss")(
        *state, own, row_biome, growth_rates)
    edge, fwd, bwd = call(
        edge_pack, (near(NF * ROWS, COLS), near(ROWS_FWD, COLS), near(ROWS_BWD, COLS)), "vvvvv"
    )(own, inner, outer, held(fwd), held(bwd))
    edge = held(edge)
    table = held(call(rate_table, (near(NTR * NTR * ROWS, COLS),), "vs")(edge, reaction_rates)[0])
    lat_s = held(lax.ppermute(fwd, "lat", [(i, i + 1) for i in range(lat - 1)]))
    lat_n = held(lax.ppermute(bwd, "lat", [(i + 1, i) for i in range(lat - 1)]))

    def body(*refs):
        step(lat * ROWS, *refs)

    outs = call(
        body,
        (far(2 * K * ROWS, COLS), far(K * ROWS, COLS), far(2 * K * ROWS, COLS), far(NTR * K * ROWS, COLS), far(K * ROWS, COLS)),
        "vvvvvssvvvv",
        scratch=[
            pltpu.VMEM((NF, 24, COLS), F32),
            pltpu.VMEM((4, 24, COLS), F32),
            pltpu.VMEM((NF + 4 + NTR, ROWS, COLS), F32),
            pltpu.VMEM((NTR * K, COLS), F32),
            pltpu.VMEM((NTR * K, COLS), F32),
            pltpu.VMEM((6, ROWS, COLS), F32),
            pltpu.VMEM((NTR * K * ROWS, COLS), F32),
            pltpu.VMEM((8, K * ROWS, COLS), F32),
        ],
    )(*state, row_biome, growth_rates, table, lat_s, lat_n, edge)
    new_vel, new_thk, new_hyd, new_trc, absorbed = outs
    return (new_vel.reshape(velocity.shape), new_thk.reshape(thickness.shape), new_hyd.reshape(hydrography.shape),
            new_trc.reshape(tracers.shape), absorbed.reshape(thickness.shape))


def solution(mesh):
    field = P(None, "lat", "lon")
    fields = P(None, None, "lat", "lon")
    in_specs = (fields, field, fields, fields, P("lat", "lon"), P("lat", "lon"), P("lat"), P(), P())
    out_specs = (fields, field, fields, fields, field)
    return jax.shard_map(per_device, mesh=mesh, in_specs=in_specs, out_specs=out_specs, check_vma=False)
```

```python
import jax
import jax.numpy as jnp
from jax import lax
from jax.experimental import pallas as pl
from jax.experimental.pallas import tpu as pltpu
from jax.sharding import PartitionSpec as P

F32 = jnp.float32
NSUB = 2
SUB = 1.0 / NSUB
NTR = 17
K = 8
ROWS = 8
COLS = 128
FU, FV, FH, FT, FS, FD = 17, 18, 19, 20, 21, 22
NF = 24
GROUP = 2
PAIRS = NF // 2
B_A, B_B, B_DA, B_DB, B_C = 0, 17, 34, 39, 44
N_FWD, N_BWD = 47, 46
C_FWD, C_BWD = N_FWD * K, N_BWD * K
ROWS_FWD, ROWS_BWD = C_FWD + 40, C_BWD + 40


def lanes(shape):
    return lax.broadcasted_iota(jnp.int32, shape, len(shape) - 1)


def subs(shape):
    return lax.broadcasted_iota(jnp.int32, shape, len(shape) - 2)


def growth_of(biome_ref, rates_ref, row):
    kind = biome_ref[row]
    rate = rates_ref[0]
    for i in range(1, rates_ref.shape[0]):
        rate = jnp.where(kind == i, rates_ref[i], rate)
    return rate


def layer_rows(ref, plane, row):
    return ref[pl.ds(plane * ROWS + row, K, stride=ROWS), :]


def lat_pack(vel, thk, hyd, trc, depth_ref, grow, after, fwd, bwd):
    depth = depth_ref[...]
    sub = subs((ROWS, COLS))

    def put(out, block, value):
        out[pl.ds(block * K, K), :] = value

    def state(out, block, row):
        put(out, block, layer_rows(vel, 0, row))
        put(out, block + 1, layer_rows(vel, K, row))
        put(out, block + 2, layer_rows(thk, 0, row))
        put(out, block + 3, layer_rows(hyd, 0, row))
        put(out, block + 4, layer_rows(hyd, K, row))

    for out, a, b in ((fwd, ROWS - 1, ROWS - 2), (bwd, 0, 1)):
        for t in range(NTR):
            put(out, B_A + t, layer_rows(trc, t * K, a))
            put(out, B_B + t, layer_rows(trc, t * K, b))
        state(out, B_DA, a)
        state(out, B_DB, b)
    put(fwd, B_C, layer_rows(vel, K, ROWS - 3))
    put(fwd, B_C + 1, layer_rows(thk, 0, ROWS - 3))
    put(bwd, B_C, layer_rows(thk, 0, 2))
    put(fwd, N_FWD - 1, jnp.where(sub == 3, grow[ROWS - 1:ROWS, :], depth))
    put(bwd, N_BWD - 1, jnp.where(sub == 3, grow[0:1, :], depth))


def lon_pack(vel_in, thk_in, hyd_in, trc_in, land, bottom, biome, rates, vel, thk, hyd, trc, depth_out, grow, out):
    for src, dst in ((trc_in, trc), (vel_in, vel), (hyd_in, hyd), (thk_in, thk)):
        dst[...] = src[...]
    depth = (land[...] * bottom[...]).astype(F32)
    depth_out[...] = depth
    sub = subs((ROWS, COLS))
    grow_tile = jnp.zeros((ROWS, COLS), F32)
    for r in range(ROWS):
        grow_tile = jnp.where(sub == r, growth_of(biome, rates, r), grow_tile)
    grow[...] = grow_tile
    group = lanes((ROWS, COLS)) >> 3

    def plane(f, k):
        if f < NTR:
            return trc_in[pl.ds((f * K + k) * ROWS, ROWS), :]
        if f < FH:
            return vel_in[pl.ds(((f - FU) * K + k) * ROWS, ROWS), :]
        if f == FH:
            return thk_in[pl.ds(k * ROWS, ROWS), :]
        if f < FD:
            return hyd_in[pl.ds(((f - FT) * K + k) * ROWS, ROWS), :]
        return depth

    for p in range(PAIRS):
        packed = jnp.zeros((ROWS, COLS), F32)
        for half in range(2):
            f = p + PAIRS * half
            if f > FD:
                continue
            for k in range(K):
                moved = pltpu.roll(plane(f, k), (half * 64 + (7 - k) * 8 + 4) % COLS, 1)
                packed = jnp.where(group == half * 8 + 7 - k, moved, packed)
        out[pl.ds(p * ROWS, ROWS), :] = packed


def edge_pack(own, inner, outer, fwd_in, bwd_in, edge, fwd, bwd):
    lane = lanes((ROWS, COLS))
    low = (lane & 7) < 4
    left = lane < 64
    odd = jnp.full((ROWS, COLS), lax.axis_index("lon") & 1) == 1
    for p in range(PAIRS):
        at = pl.ds(p * ROWS, ROWS)
        o, a, b = own[at, :], inner[at, :], outer[at, :]
        x = jnp.where(low, jnp.where(odd, a, b), o)
        y = jnp.where(low, o, jnp.where(odd, b, a))
        edge[pl.ds(p * ROWS, ROWS), :] = jnp.where(left, x, pltpu.roll(y, 64, 1))
        edge[pl.ds((p + PAIRS) * ROWS, ROWS), :] = jnp.where(left, pltpu.roll(x, 64, 1), y)
    for out, source, at, a, b, c in ((fwd, fwd_in, C_FWD, 7, 6, 5), (bwd, bwd_in, C_BWD, 0, 1, 2)):
        out[pl.ds(0, at), :] = source[...]
        for i in range(3):
            out[pl.ds(at + i * 8, 8), :] = edge[pl.ds(i * 64 + a, 8, stride=8), :]
        out[pl.ds(at + 24, 8), :] = edge[pl.ds(128 + b, 8, stride=8), :]
        out[pl.ds(at + 32, 8), :] = edge[pl.ds(128 + c, 8, stride=8), :]


def kappa_of(wet, below):
    return wet * (0.02 + 0.1 / (1.0 + 10.0 * below * below))


def density(t, s):
    return 0.25 * s - 0.2 * t


def laplace(a, ae, aw, an, as_, we, ww, wn, ws):
    return we * (ae - a) - ww * (a - aw) + wn * (an - a) - ws * (a - as_)


def parts(transport, diffuse):
    return jnp.maximum(transport, 0.0) + diffuse, jnp.minimum(transport, 0.0) - diffuse


def step_weights(te, de, tw, dw, tn, dn, ts, ds):
    ae, be = parts(te, de)
    aw, bw = parts(tw, dw)
    an, bn = parts(tn, dn)
    as_, bs = parts(ts, ds)
    return 1.0 - SUB * (ae - bw + an - bs), -SUB * be, SUB * aw, -SUB * bn, SUB * as_


def react(adv, rate_at, wet, gain, store):
    react_all([adv], rate_at, [wet], [gain], lambda i, t, value: store(t, value))


def react_all(cells, rate_at, wets, gains, store):
    uptakes = []
    for adv, gain in zip(cells, gains):
        square = adv[0] * adv[0]
        uptakes.append(gain * adv[1] * square / (1.0 + square))
    for t in range(NTR):
        totals = [adv[t] for adv in cells]
        for s in range(NTR):
            rate = rate_at(t, s)
            totals = [total + rate * adv[s] for total, adv in zip(totals, cells)]
        for i, total in enumerate(totals):
            if t == 0:
                total = total - uptakes[i]
            if t == 1:
                total = total + uptakes[i]
            store(i, t, wets[i] * total)


def step(total_rows, vel, thk, hyd, trc, depth_ref, grow, table, lat_s, lat_n, edge,
         out_vel, out_thk, out_hyd, out_trc, out_abs,
         ex, es, mp, l1s, l1n, lw, c1, cf):
    first = (lax.axis_index("lat") * ROWS).astype(F32)

    def latitude(row):
        return 2.0 * (first + row + 0.5) / total_rows - 1.0

    def rate_at(t, s):
        return table[pl.ds((t * NTR + s) * ROWS, ROWS), :]

    lane = lanes((ROWS, COLS))
    sub = subs((ROWS, COLS))
    at_first, at_last = lane == 0, lane == COLS - 1
    top_row, end_row = sub == 0, sub == ROWS - 1

    def mprime(value):
        return jnp.where((lane & 7) == 5, pltpu.roll(value, 2, 1), pltpu.roll(value, 64, 1))

    cor_s = lat_s.at[pl.ds(C_FWD, 40), :]
    cor_n = lat_n.at[pl.ds(C_BWD, 40), :]

    for f in range(NF - 1):
        own = edge[pl.ds(f * ROWS, ROWS), :]
        mp[f] = mprime(own)
        if f >= NTR:
            ex[f, 0:8, :] = jnp.zeros((8, COLS), F32)
            ex[f, 16:24, :] = jnp.zeros((8, COLS), F32)
            for i, at in ((1, 24), (2, 32)):
                ex[f, 7 - i:8 - i, :] = cor_s[at + f - 16:at + f - 15, :]
                ex[f, 16 + i:17 + i, :] = cor_n[at + f - 16:at + f - 15, :]
        ex[f, 7:8, :] = cor_s[f:f + 1, :]
        ex[f, 16:17, :] = cor_n[f:f + 1, :]
        ex[f, 8:16, :] = own

    def east(a):
        return pltpu.roll(a, COLS - 1, 1)

    def west(a):
        return pltpu.roll(a, 1, 1)

    def north(a):
        return pltpu.roll(a, 23, 0)

    def south(a):
        return pltpu.roll(a, 1, 0)

    big = (24, COLS)
    layer = 7 - ((lanes(big) >> 3) & 7)
    u, v, h, t_, s_ = ex[FU], ex[FV], ex[FH], ex[FT], ex[FS]
    wet = (layer.astype(F32) < ex[FD]).astype(F32)
    rho = density(t_, s_)
    p = 0.3 * h + rho
    cor = 0.3 * latitude((subs(big) - 8).astype(F32))
    we = wet * east(wet)
    wn = wet * north(wet)
    ww, ws = west(we), south(wn)
    lap_u = laplace(u, east(u), west(u), north(u), south(u), we, ww, wn, ws)
    lap_v = laplace(v, east(v), west(v), north(v), south(v), we, ww, wn, ws)
    new_u = we * (u + cor * v - (east(p) - p) + 0.1 * lap_u)
    new_v = wn * (v - cor * u - (north(p) - p) + 0.1 * lap_v)
    qe = we * u * 0.5 * (h + east(h))
    qn = wn * v * 0.5 * (h + north(h))
    new_h = wet * (h - (qe - west(qe) + qn - south(qn)))
    kap = kappa_of(wet, jnp.where(layer < K - 1, pltpu.roll(rho, 8, 1) - rho, 0.0))
    te = new_u * 0.5 * (new_h + east(new_h))
    tn = new_v * 0.5 * (new_h + north(new_h))
    de = we * 0.5 * (kap + east(kap))
    dn = wn * 0.5 * (kap + north(kap))
    for i, value in enumerate((new_h, kap, te, de)):
        es[i] = value
        mp[FD + 1 + i] = mprime(value[8:16])
    weights = step_weights(te, de, west(te), west(de), tn, dn, south(tn), south(dn))
    weights = [w[8:16] for w in weights]
    small_layer = 7 - ((lane >> 3) & 7)
    wet8 = wet[8:16]
    chl = ex[1, 8:16, :]
    att = wet8 * (0.1 + 0.2 * chl * chl)
    total = att
    for shift in (1, 2, 4):
        total = total + jnp.where(small_layer >= shift, pltpu.roll(total, COLS - 8 * shift, 1), 0.0)
    lat8 = latitude(sub.astype(F32))
    sun8 = 1.0 - 0.8 * lat8 * lat8
    grow8 = grow[...]
    gain = SUB * grow8 * sun8 * jnp.exp(-(total - att))
    adv = []
    for t in range(NTR):
        c = ex[t, 8:16, :]
        w0, w1, w2, w3, w4 = weights
        adv.append(w0 * c + w1 * east(c) + w2 * west(c) + w3 * ex[t, 9:17, :] + w4 * ex[t, 7:15, :])

    def keep_edge(t, value):
        mp[NF + 4 + t] = mprime(value)

    react(adv, rate_at, wet8, gain, keep_edge)

    def layered(row):
        return jnp.broadcast_to(row, (K, COLS))

    def from_west(row):
        return pltpu.roll(layered(row), 69, 1, stride=8, stride_axis=0)

    def from_east(row):
        return pltpu.roll(layered(row), 3, 1, stride=8, stride_axis=0)

    def lat_east(a, row):
        return jnp.where(at_last, from_east(row), east(a))

    def lat_west(a, row):
        return jnp.where(at_first, from_west(row), west(a))

    kf = sub.astype(F32)
    own_depth = depth_ref[...]

    def block(ref, i):
        return ref[pl.ds(i * K, K), :]

    class Line:
        pass

    def line(ref, misc, base, er, depth_row):
        o = Line()
        o.u, o.v, o.h, o.t, o.s = (block(ref, base + i) for i in range(5))
        o.wet = (kf < layered(ref[misc * K + depth_row:misc * K + depth_row + 1, :])).astype(F32)
        o.er = er
        return around(o)

    def around(o):
        er = o.er
        o.p = 0.3 * o.h + density(o.t, o.s)

        def e(f):
            return ex[f, er:er + 1, :]

        o.ue, o.uw = lat_east(o.u, e(FU)), lat_west(o.u, e(FU))
        o.ve, o.vw = lat_east(o.v, e(FV)), lat_west(o.v, e(FV))
        o.he, o.hw = lat_east(o.h, e(FH)), lat_west(o.h, e(FH))
        pe = 0.3 * e(FH) + density(e(FT), e(FS))
        o.pe = lat_east(o.p, pe)
        wet_e = (kf < from_east(e(FD))).astype(F32)
        wet_w = (kf < from_west(e(FD))).astype(F32)
        o.we = o.wet * jnp.where(at_last, wet_e, east(o.wet))
        o.ww = o.wet * jnp.where(at_first, wet_w, west(o.wet))
        rho = density(o.t, o.s)
        o.kap = kappa_of(o.wet, jnp.where(sub < K - 1, pltpu.roll(rho, K - 1, 0) - rho, 0.0))
        return o

    def own_line(row):
        o = Line()
        o.u, o.v, o.h = layer_rows(vel, 0, row), layer_rows(vel, K, row), layer_rows(thk, 0, row)
        o.p = 0.3 * o.h + density(layer_rows(hyd, 0, row), layer_rows(hyd, K, row))
        o.wet = (kf < layered(depth_ref[row:row + 1, :])).astype(F32)
        return o

    def height(o, n, s):
        wn, ws = o.wet * n.wet, o.wet * s.wet
        qe = o.we * o.u * 0.5 * (o.h + o.he)
        qw = o.ww * o.uw * 0.5 * (o.hw + o.h)
        qn = wn * o.v * 0.5 * (o.h + n.h)
        qs = ws * s.v * 0.5 * (s.h + o.h)
        return o.wet * (o.h - (qe - qw + qn - qs))

    def east_speed(o, n, s, cor):
        wn, ws = o.wet * n.wet, o.wet * s.wet
        return o.we * (o.u + cor * o.v - (o.pe - o.p) + 0.1 * laplace(o.u, o.ue, o.uw, n.u, s.u, o.we, o.ww, wn, ws))

    def north_speed(o, n, s, cor):
        wn, ws = o.wet * n.wet, o.wet * s.wet
        return wn * (o.v - cor * o.u - (n.p - o.p) + 0.1 * laplace(o.v, o.ve, o.vw, n.v, s.v, o.we, o.ww, wn, ws))

    sa = line(lat_s, N_FWD - 1, B_DA, 7, 7)
    sb = line(lat_s, N_FWD - 1, B_DB, 6, 6)
    sc = Line()
    sc.v, sc.h = block(lat_s, B_C), block(lat_s, B_C + 1)
    sc.wet = (kf < layered(lat_s[(N_FWD - 1) * K + 5:(N_FWD - 1) * K + 6, :])).astype(F32)
    na = line(lat_n, N_BWD - 1, B_DA, 16, 0)
    nb = line(lat_n, N_BWD - 1, B_DB, 17, 1)
    nc = Line()
    nc.h = block(lat_n, B_C)
    nc.wet = (kf < layered(lat_n[(N_BWD - 1) * K + 2:(N_BWD - 1) * K + 3, :])).astype(F32)
    row0, row7 = own_line(0), own_line(ROWS - 1)

    sa.nu = east_speed(sa, row0, sb, 0.3 * latitude(-1.0))
    sa.nv = north_speed(sa, row0, sb, 0.3 * latitude(-1.0))
    sa.nh = height(sa, row0, sb)
    sb.nv = north_speed(sb, sa, sc, 0.3 * latitude(-2.0))
    sb.nh = height(sb, sa, sc)
    na.nu = east_speed(na, nb, row7, 0.3 * latitude(float(ROWS)))
    na.nv = north_speed(na, nb, row7, 0.3 * latitude(float(ROWS)))
    na.nh = height(na, nb, row7)
    nb.nh = height(nb, nc, na)
    for i, value in enumerate((sa.nv, sa.nh, sa.kap, na.nh, na.kap)):
        lw[1 + i] = value

    lat_col = latitude(sub.astype(F32))
    cor8 = 0.3 * lat_col
    depth_mp = mp[FD]

    def row_of(ref, at):
        return jnp.broadcast_to(ref[pl.ds(at, 1), :], (ROWS, COLS))

    def around_sides(value, f, shift):
        edge_value = pltpu.roll(mp[f], shift, 1)
        return jnp.where(at_last, edge_value, east(value)), jnp.where(at_first, edge_value, west(value))

    def around_ends(value, rn, rs):
        return jnp.where(end_row, rn, pltpu.roll(value, ROWS - 1, 0)), jnp.where(top_row, rs, pltpu.roll(value, 1, 0))

    dep_e, dep_w = around_sides(own_depth, FD, 67)
    dep_n, dep_s = around_ends(own_depth, row_of(lat_n, (N_BWD - 1) * K), row_of(lat_s, (N_FWD - 1) * K + 7))

    def cells(k, over):
        shift = 67 + 8 * k
        kk = k.astype(F32)
        at = pl.ds(pl.multiple_of(k * ROWS, ROWS), ROWS)
        at2 = pl.ds(pl.multiple_of((k + K) * ROWS, ROWS), ROWS)
        u, v, h, t_, s_ = vel[at, :], vel[at2, :], thk[at, :], hyd[at, :], hyd[at2, :]
        wet = (kk < own_depth).astype(F32)
        we = wet * (kk < dep_e).astype(F32)
        ww = wet * (kk < dep_w).astype(F32)
        wn = wet * (kk < dep_n).astype(F32)
        ws = wet * (kk < dep_s).astype(F32)

        def near(value, f, i):
            e, w = around_sides(value, f, shift)
            n, s = around_ends(value, row_of(lat_n, (B_DA + i) * K + k), row_of(lat_s, (B_DA + i) * K + k))
            return e, w, n, s

        ue, uw, un, us = near(u, FU, 0)
        ve, vw, vn, vs = near(v, FV, 1)
        he, hw, hn, hs = near(h, FH, 2)
        t_e, tw, t_n, ts = near(t_, FT, 3)
        s_e, sw, s_n, ss = near(s_, FS, 4)
        p = 0.3 * h + density(t_, s_)
        pe = 0.3 * he + density(t_e, s_e)
        pn = 0.3 * hn + density(t_n, s_n)
        nu = we * (u + cor8 * v - (pe - p) + 0.1 * laplace(u, ue, uw, un, us, we, ww, wn, ws))
        nv = wn * (v - cor8 * u - (pn - p) + 0.1 * laplace(v, ve, vw, vn, vs, we, ww, wn, ws))
        qe = we * u * 0.5 * (h + he)
        qw = ww * uw * 0.5 * (hw + h)
        qn = wn * v * 0.5 * (h + hn)
        qs = ws * vs * 0.5 * (hs + h)
        nh = wet * (h - (qe - qw + qn - qs))
        out_vel[at, :] = nu
        out_vel[at2, :] = nv
        out_thk[at, :] = nh
        lower = jnp.minimum(k + 1, K - 1)
        al = pl.ds(pl.multiple_of(lower * ROWS, ROWS), ROWS)
        al2 = pl.ds(pl.multiple_of((lower + K) * ROWS, ROWS), ROWS)
        below = density(hyd[al, :], hyd[al2, :]) - density(t_, s_)
        kap = kappa_of(wet, below)
        chl = trc[pl.ds(pl.multiple_of((k + K) * ROWS, ROWS), ROWS), :]
        att = wet * (0.1 + 0.2 * chl * chl)
        light = sun8 * jnp.exp(-over)
        absorbed = light * (1.0 - jnp.exp(-att))
        out_abs[at, :] = absorbed
        out_hyd[at, :] = wet * (t_ + 0.1 * laplace(t_, t_e, tw, t_n, ts, we, ww, wn, ws)) + absorbed
        out_hyd[at2, :] = wet * (s_ + 0.1 * laplace(s_, s_e, sw, s_n, ss, we, ww, wn, ws))
        nhe = jnp.where(at_last, pltpu.roll(mp[FD + 1], shift, 1), east(nh))
        kape = jnp.where(at_last, pltpu.roll(mp[FD + 2], shift, 1), east(kap))
        nhn = jnp.where(end_row, row_of(lw.at[4], k), pltpu.roll(nh, ROWS - 1, 0))
        kapn = jnp.where(end_row, row_of(lw.at[5], k), pltpu.roll(kap, ROWS - 1, 0))
        te = nu * 0.5 * (nh + nhe)
        de = we * 0.5 * (kap + kape)
        tn = nv * 0.5 * (nh + nhn)
        dn = wn * 0.5 * (kap + kapn)
        tw = jnp.where(at_first, pltpu.roll(mp[FD + 3], shift, 1), west(te))
        dw = jnp.where(at_first, pltpu.roll(mp[FD + 4], shift, 1), west(de))
        ts = jnp.where(top_row, row_of(lw.at[1], k) * 0.5 * (row_of(lw.at[2], k) + nh), pltpu.roll(tn, 1, 0))
        ds = jnp.where(top_row, ws * 0.5 * (row_of(lw.at[3], k) + kap), pltpu.roll(dn, 1, 0))
        for i, w in enumerate(step_weights(te, de, tw, dw, tn, dn, ts, ds)):
            cf[i, at, :] = w
        cf[5, at, :] = SUB * grow8 * light
        cf[6, at, :] = tn
        cf[7, at, :] = dn
        return over + att

    lax.fori_loop(0, K, cells, jnp.zeros((ROWS, COLS), F32))

    def outer(o, te_row, grow, lat_row, tn, dn, ts, ds, near_ref, north_of, south_of, er, kept):
        he = lat_east(o.nh, es[0, er:er + 1, :])
        kape = lat_east(o.kap, es[1, er:er + 1, :])
        te = o.nu * 0.5 * (o.nh + he)
        de = o.we * 0.5 * (o.kap + kape)
        tw = lat_west(te, es[2, er:er + 1, :])
        dw = lat_west(de, es[3, er:er + 1, :])
        w0, w1, w2, w3, w4 = step_weights(te, de, tw, dw, tn, dn, ts, ds)
        chl = block(near_ref, B_A + 1)
        att = o.wet * (0.1 + 0.2 * chl * chl)
        total = att
        for shift in (1, 2, 4):
            total = total + jnp.where(sub >= shift, pltpu.roll(total, shift, 0), 0.0)
        lat_here = latitude(lat_row)
        gain = SUB * layered(grow) * ((1.0 - 0.8 * lat_here * lat_here) * jnp.exp(-(total - att)))
        adv = []
        for t in range(NTR):
            c = block(near_ref, B_A + t)
            row = ex[t, er:er + 1, :]
            adv.append(w0 * c + w1 * lat_east(c, row) + w2 * lat_west(c, row) + w3 * north_of(t) + w4 * south_of(t))

        def keep(t, value):
            kept[pl.ds(t * K, K), :] = value

        react(adv, rate_at, o.wet, gain, keep)

    h0 = layer_rows(out_thk, 0, 0)
    kap0 = kappa_of(row0.wet, row_below(hyd, 0, sub))
    wn_s = sa.wet * row0.wet
    outer(sa, None, lat_s[(N_FWD - 1) * K + 3:(N_FWD - 1) * K + 4, :], -1.0,
          sa.nv * 0.5 * (sa.nh + h0), wn_s * 0.5 * (sa.kap + kap0),
          sb.nv * 0.5 * (sb.nh + sa.nh), sb.wet * sa.wet * 0.5 * (sb.kap + sa.kap),
          lat_s, lambda t: layer_rows(trc, t * K, 0), lambda t: block(lat_s, B_B + t), 7, l1s)
    outer(na, None, lat_n[(N_BWD - 1) * K + 3:(N_BWD - 1) * K + 4, :], float(ROWS),
          na.nv * 0.5 * (na.nh + nb.nh), na.wet * nb.wet * 0.5 * (na.kap + nb.kap),
          layer_rows(cf.at[6], 0, ROWS - 1), layer_rows(cf.at[7], 0, ROWS - 1),
          lat_n, lambda t: block(lat_n, B_B + t), lambda t: layer_rows(trc, t * K, ROWS - 1), 16, l1n)

    def substep(src, dst, mp_base, end_n, end_s):
        def advect(k):
            shift = 67 + 8 * k
            at = pl.ds(pl.multiple_of(k * ROWS, ROWS), ROWS)
            w0, w1, w2, w3, w4 = (cf[i, at, :] for i in range(5))
            adv = []
            for t in range(NTR):
                c = src[pl.ds(pl.multiple_of((t * K + k) * ROWS, ROWS), ROWS), :]
                e, w = around_sides(c, mp_base + t, shift)
                n, s = around_ends(c, row_of(end_n, t * K + k), row_of(end_s, t * K + k))
                adv.append(w0 * c + w1 * e + w2 * w + w3 * n + w4 * s)
            return adv, (k.astype(F32) < own_depth).astype(F32), cf[5, at, :]

        def body(j, carry):
            ks = [GROUP * j + i for i in range(GROUP)]
            cells, wets, gains = zip(*(advect(k) for k in ks))

            def keep(i, t, value):
                dst[pl.ds(pl.multiple_of((t * K + ks[i]) * ROWS, ROWS), ROWS), :] = value

            react_all(cells, rate_at, wets, gains, keep)
            return carry

        lax.fori_loop(0, K // GROUP, body, 0)

    substep(trc, c1, 0, lat_n, lat_s)
    substep(c1, out_trc, NF + 4, l1n, l1s)


def row_below(hyd, row, sub):
    rho = density(layer_rows(hyd, 0, row), layer_rows(hyd, K, row))
    return jnp.where(sub < K - 1, pltpu.roll(rho, K - 1, 0) - rho, 0.0)


def rate_table(after, rr, out):
    for t in range(NTR):
        for s in range(NTR):
            out[pl.ds((t * NTR + s) * ROWS, ROWS), :] = jnp.full((ROWS, COLS), SUB * rr[t, s])


def near(*dims):
    return pltpu.VMEM(dims, F32)


def far(*dims):
    return jax.ShapeDtypeStruct(dims, F32)


def held(x):
    return pltpu.with_memory_space_constraint(x, pltpu.VMEM)


def call(kernel, out_shape, spaces, scratch=(), flops=100000):
    spec = {"a": pl.BlockSpec(memory_space=pl.ANY), "v": pl.BlockSpec(memory_space=pltpu.VMEM), "s": pl.BlockSpec(memory_space=pltpu.SMEM)}
    return pl.pallas_call(
        kernel,
        out_shape=out_shape,
        in_specs=[spec[c] for c in spaces],
        out_specs=tuple(spec["v"] for _ in out_shape),
        scratch_shapes=list(scratch),
        cost_estimate=pl.CostEstimate(flops=flops, bytes_accessed=100000, transcendentals=0),
    )


def per_device(velocity, thickness, hydrography, tracers, land_mask, bottom_layer, row_biome, reaction_rates, growth_rates):
    lat, lon = lax.axis_size("lat"), lax.axis_size("lon")
    vel = velocity.reshape(2 * K * ROWS, COLS)
    thk = thickness.reshape(K * ROWS, COLS)
    hyd = hydrography.reshape(2 * K * ROWS, COLS)
    trc = tracers.reshape(NTR * K * ROWS, COLS)

    def swap(n, start):
        return [p for i in range(start, n - 1, 2) for p in ((i, i + 1), (i + 1, i))]

    *state, own = (held(x) for x in call(
        lon_pack,
        (near(2 * K * ROWS, COLS), near(K * ROWS, COLS), near(2 * K * ROWS, COLS), near(NTR * K * ROWS, COLS),
         near(ROWS, COLS), near(ROWS, COLS), near(PAIRS * ROWS, COLS)),
        "vvvvvvss",
    )(vel, thk, hyd, trc, land_mask, bottom_layer, row_biome, growth_rates))
    outer = held(lax.ppermute(own, "lon", swap(lon, 1)))
    inner = held(lax.ppermute(own, "lon", swap(lon, 0)))
    fwd, bwd = call(lat_pack, (near(C_FWD, COLS), near(C_BWD, COLS)), "vvvvvvv")(
        *state, own)
    edge, fwd, bwd = call(
        edge_pack, (near(NF * ROWS, COLS), near(ROWS_FWD, COLS), near(ROWS_BWD, COLS)), "vvvvv"
    )(own, inner, outer, held(fwd), held(bwd))
    edge = held(edge)
    table = held(call(rate_table, (near(NTR * NTR * ROWS, COLS),), "vs")(edge, reaction_rates)[0])
    lat_s = held(lax.ppermute(fwd, "lat", [(i, i + 1) for i in range(lat - 1)]))
    lat_n = held(lax.ppermute(bwd, "lat", [(i + 1, i) for i in range(lat - 1)]))

    def body(*refs):
        step(lat * ROWS, *refs)

    outs = call(
        body,
        (far(2 * K * ROWS, COLS), far(K * ROWS, COLS), far(2 * K * ROWS, COLS), far(NTR * K * ROWS, COLS), far(K * ROWS, COLS)),
        "vvvvvvvvvv",
        scratch=[
            pltpu.VMEM((NF, 24, COLS), F32),
            pltpu.VMEM((4, 24, COLS), F32),
            pltpu.VMEM((NF + 4 + NTR, ROWS, COLS), F32),
            pltpu.VMEM((NTR * K, COLS), F32),
            pltpu.VMEM((NTR * K, COLS), F32),
            pltpu.VMEM((6, ROWS, COLS), F32),
            pltpu.VMEM((NTR * K * ROWS, COLS), F32),
            pltpu.VMEM((8, K * ROWS, COLS), F32),
        ],
    )(*state, table, lat_s, lat_n, edge)
    new_vel, new_thk, new_hyd, new_trc, absorbed = outs
    return (new_vel.reshape(velocity.shape), new_thk.reshape(thickness.shape), new_hyd.reshape(hydrography.shape),
            new_trc.reshape(tracers.shape), absorbed.reshape(thickness.shape))


def solution(mesh):
    field = P(None, "lat", "lon")
    fields = P(None, None, "lat", "lon")
    in_specs = (fields, field, fields, fields, P("lat", "lon"), P("lat", "lon"), P("lat"), P(), P())
    out_specs = (fields, field, fields, fields, field)
    return jax.shard_map(per_device, mesh=mesh, in_specs=in_specs, out_specs=out_specs, check_vma=False)
```

```python
import jax
import jax.numpy as jnp
from jax import lax
from jax.experimental import pallas as pl
from jax.experimental.pallas import tpu as pltpu
from jax.sharding import PartitionSpec as P

F32 = jnp.float32
NSUB = 2
SUB = 1.0 / NSUB
NTR = 17
K = 8
ROWS = 8
COLS = 128
FU, FV, FH, FT, FS, FD = 17, 18, 19, 20, 21, 22
NF = 24
GROUP = 2
PAIRS = NF // 2
B_A, B_B, B_DA, B_DB, B_C = 0, 17, 34, 39, 44
N_FWD, N_BWD = 47, 46
C_FWD, C_BWD = N_FWD * K, N_BWD * K
ROWS_FWD, ROWS_BWD = C_FWD + 24, C_BWD + 24


def lanes(shape):
    return lax.broadcasted_iota(jnp.int32, shape, len(shape) - 1)


def subs(shape):
    return lax.broadcasted_iota(jnp.int32, shape, len(shape) - 2)


def growth_of(biome_ref, rates_ref, row):
    kind = biome_ref[row]
    rate = rates_ref[0]
    for i in range(1, rates_ref.shape[0]):
        rate = jnp.where(kind == i, rates_ref[i], rate)
    return rate


def layer_rows(ref, plane, row):
    return ref[pl.ds(plane * ROWS + row, K, stride=ROWS), :]


def lat_pack(vel, thk, hyd, trc, depth_ref, grow, after, fwd, bwd):
    depth = depth_ref[...]
    sub = subs((ROWS, COLS))

    def put(out, block, value):
        out[pl.ds(block * K, K), :] = value

    def state(out, block, row):
        put(out, block, layer_rows(vel, 0, row))
        put(out, block + 1, layer_rows(vel, K, row))
        put(out, block + 2, layer_rows(thk, 0, row))
        put(out, block + 3, layer_rows(hyd, 0, row))
        put(out, block + 4, layer_rows(hyd, K, row))

    for out, a, b in ((fwd, ROWS - 1, ROWS - 2), (bwd, 0, 1)):
        for t in range(NTR):
            put(out, B_A + t, layer_rows(trc, t * K, a))
            put(out, B_B + t, layer_rows(trc, t * K, b))
        state(out, B_DA, a)
        state(out, B_DB, b)
    put(fwd, B_C, layer_rows(vel, K, ROWS - 3))
    put(fwd, B_C + 1, layer_rows(thk, 0, ROWS - 3))
    put(bwd, B_C, layer_rows(thk, 0, 2))
    put(fwd, N_FWD - 1, jnp.where(sub == 3, grow[ROWS - 1:ROWS, :], depth))
    put(bwd, N_BWD - 1, jnp.where(sub == 3, grow[0:1, :], depth))


def lon_pack(vel_in, thk_in, hyd_in, trc_in, land, bottom, biome, rates, vel, thk, hyd, trc, depth_out, grow, out):
    for src, dst in ((trc_in, trc), (vel_in, vel), (hyd_in, hyd), (thk_in, thk)):
        dst[...] = src[...]
    depth = (land[...] * bottom[...]).astype(F32)
    depth_out[...] = depth
    sub = subs((ROWS, COLS))
    grow_tile = jnp.zeros((ROWS, COLS), F32)
    for r in range(ROWS):
        grow_tile = jnp.where(sub == r, growth_of(biome, rates, r), grow_tile)
    grow[...] = grow_tile
    group = lanes((ROWS, COLS)) >> 3

    def plane(f, k):
        if f < NTR:
            return trc_in[pl.ds((f * K + k) * ROWS, ROWS), :]
        if f < FH:
            return vel_in[pl.ds(((f - FU) * K + k) * ROWS, ROWS), :]
        if f == FH:
            return thk_in[pl.ds(k * ROWS, ROWS), :]
        if f < FD:
            return hyd_in[pl.ds(((f - FT) * K + k) * ROWS, ROWS), :]
        return depth

    for p in range(PAIRS):
        packed = jnp.zeros((ROWS, COLS), F32)
        for half in range(2):
            f = p + PAIRS * half
            if f > FD:
                continue
            for k in range(K):
                moved = pltpu.roll(plane(f, k), (half * 64 + (7 - k) * 8 + 4) % COLS, 1)
                packed = jnp.where(group == half * 8 + 7 - k, moved, packed)
        out[pl.ds(p * ROWS, ROWS), :] = packed


def edge_pack(own, inner, outer, fwd_in, bwd_in, edge, fwd, bwd):
    lane = lanes((ROWS, COLS))
    low = (lane & 7) < 4
    left = lane < 64
    odd = jnp.full((ROWS, COLS), lax.axis_index("lon") & 1) == 1
    for p in range(PAIRS):
        at = pl.ds(p * ROWS, ROWS)
        o, a, b = own[at, :], inner[at, :], outer[at, :]
        x = jnp.where(low, jnp.where(odd, a, b), o)
        y = jnp.where(low, o, jnp.where(odd, b, a))
        edge[pl.ds(p * ROWS, ROWS), :] = jnp.where(left, x, pltpu.roll(y, 64, 1))
        edge[pl.ds((p + PAIRS) * ROWS, ROWS), :] = jnp.where(left, pltpu.roll(x, 64, 1), y)
    place = lane & 7
    corners = []
    for i in range(3):
        packed = jnp.zeros((ROWS, COLS), F32)
        for q in range(min(7, NTR - 7 * i)):
            moved = pltpu.roll(edge[pl.ds((7 * i + q) * ROWS, ROWS), :], (q - 3) % COLS, 1)
            packed = jnp.where(place == jnp.where(left, q, q + 1), moved, packed)
        corners.append(packed)
    for out, source, at, a, b, c in ((fwd, fwd_in, C_FWD, 7, 6, 5), (bwd, bwd_in, C_BWD, 0, 1, 2)):
        out[pl.ds(0, at), :] = source[...]
        for i, row in enumerate((a, b, c)):
            out[pl.ds(at + i * 8, 8), :] = edge[pl.ds(128 + row, 8, stride=8), :]
            out[pl.ds(at + i * 8, 1), :] = corners[i][a:a + 1, :]


def kappa_of(wet, below):
    return wet * (0.02 + 0.1 / (1.0 + 10.0 * below * below))


def density(t, s):
    return 0.25 * s - 0.2 * t


def laplace(a, ae, aw, an, as_, we, ww, wn, ws):
    return we * (ae - a) - ww * (a - aw) + wn * (an - a) - ws * (a - as_)


def parts(transport, diffuse):
    return jnp.maximum(transport, 0.0) + diffuse, jnp.minimum(transport, 0.0) - diffuse


def step_weights(te, de, tw, dw, tn, dn, ts, ds):
    ae, be = parts(te, de)
    aw, bw = parts(tw, dw)
    an, bn = parts(tn, dn)
    as_, bs = parts(ts, ds)
    return 1.0 - SUB * (ae - bw + an - bs), -SUB * be, SUB * aw, -SUB * bn, SUB * as_


def react(adv, rate_at, wet, gain, store):
    react_all([adv], rate_at, [wet], [gain], lambda i, t, value: store(t, value))


def react_all(cells, rate_at, wets, gains, store):
    uptakes = []
    for adv, gain in zip(cells, gains):
        square = adv[0] * adv[0]
        uptakes.append(gain * adv[1] * square / (1.0 + square))
    for t in range(NTR):
        totals = [adv[t] for adv in cells]
        for s in range(NTR):
            rate = rate_at(t, s)
            totals = [total + rate * adv[s] for total, adv in zip(totals, cells)]
        for i, total in enumerate(totals):
            if t == 0:
                total = total - uptakes[i]
            if t == 1:
                total = total + uptakes[i]
            store(i, t, wets[i] * total)


def step(total_rows, vel, thk, hyd, trc, depth_ref, grow, table, lat_s, lat_n, edge,
         to_vel, to_thk, to_hyd, to_trc, to_abs,
         ex, es, mp, l1s, l1n, lw, c1, cf, out_vel, out_thk, out_hyd, out_trc, out_abs, sems):
    first = (lax.axis_index("lat") * ROWS).astype(F32)

    def latitude(row):
        return 2.0 * (first + row + 0.5) / total_rows - 1.0

    def rate_at(t, s):
        return table[pl.ds((t * NTR + s) * ROWS, ROWS), :]

    lane = lanes((ROWS, COLS))
    sub = subs((ROWS, COLS))
    at_first, at_last = lane == 0, lane == COLS - 1
    top_row, end_row = sub == 0, sub == ROWS - 1

    def mprime(value):
        return jnp.where((lane & 7) == 5, pltpu.roll(value, 2, 1), pltpu.roll(value, 64, 1))

    cor_s = lat_s.at[pl.ds(C_FWD, 24), :]
    cor_n = lat_n.at[pl.ds(C_BWD, 24), :]

    for f in range(NF - 1):
        own = edge[pl.ds(f * ROWS, ROWS), :]
        mp[f] = mprime(own)
        if f >= NTR:
            ex[f, 0:8, :] = jnp.zeros((8, COLS), F32)
            ex[f, 16:24, :] = jnp.zeros((8, COLS), F32)
            for i in range(3):
                at = i * 8 + f - 16
                ex[f, 7 - i:8 - i, :] = cor_s[at:at + 1, :]
                ex[f, 16 + i:17 + i, :] = cor_n[at:at + 1, :]
        else:
            for ref, at in ((cor_s, 7), (cor_n, 16)):
                row = jnp.broadcast_to(ref[f // 7 * 8:f // 7 * 8 + 1, :], (ROWS, COLS))
                ex[f, at:at + 1, :] = pltpu.roll(row, (3 - f % 7) % COLS, 1)[0:1, :]
        ex[f, 8:16, :] = own

    def east(a):
        return pltpu.roll(a, COLS - 1, 1)

    def west(a):
        return pltpu.roll(a, 1, 1)

    def north(a):
        return pltpu.roll(a, 23, 0)

    def south(a):
        return pltpu.roll(a, 1, 0)

    big = (24, COLS)
    layer = 7 - ((lanes(big) >> 3) & 7)
    u, v, h, t_, s_ = ex[FU], ex[FV], ex[FH], ex[FT], ex[FS]
    wet = (layer.astype(F32) < ex[FD]).astype(F32)
    rho = density(t_, s_)
    p = 0.3 * h + rho
    cor = 0.3 * latitude((subs(big) - 8).astype(F32))
    we = wet * east(wet)
    wn = wet * north(wet)
    ww, ws = west(we), south(wn)
    lap_u = laplace(u, east(u), west(u), north(u), south(u), we, ww, wn, ws)
    lap_v = laplace(v, east(v), west(v), north(v), south(v), we, ww, wn, ws)
    new_u = we * (u + cor * v - (east(p) - p) + 0.1 * lap_u)
    new_v = wn * (v - cor * u - (north(p) - p) + 0.1 * lap_v)
    qe = we * u * 0.5 * (h + east(h))
    qn = wn * v * 0.5 * (h + north(h))
    new_h = wet * (h - (qe - west(qe) + qn - south(qn)))
    kap = kappa_of(wet, jnp.where(layer < K - 1, pltpu.roll(rho, 8, 1) - rho, 0.0))
    te = new_u * 0.5 * (new_h + east(new_h))
    tn = new_v * 0.5 * (new_h + north(new_h))
    de = we * 0.5 * (kap + east(kap))
    dn = wn * 0.5 * (kap + north(kap))
    for i, value in enumerate((new_h, kap, te, de)):
        es[i] = value
        mp[FD + 1 + i] = mprime(value[8:16])
    weights = step_weights(te, de, west(te), west(de), tn, dn, south(tn), south(dn))
    weights = [w[8:16] for w in weights]
    small_layer = 7 - ((lane >> 3) & 7)
    wet8 = wet[8:16]
    chl = ex[1, 8:16, :]
    att = wet8 * (0.1 + 0.2 * chl * chl)
    total = att
    for shift in (1, 2, 4):
        total = total + jnp.where(small_layer >= shift, pltpu.roll(total, COLS - 8 * shift, 1), 0.0)
    lat8 = latitude(sub.astype(F32))
    sun8 = 1.0 - 0.8 * lat8 * lat8
    grow8 = grow[...]
    gain = SUB * grow8 * sun8 * jnp.exp(-(total - att))
    adv = []
    for t in range(NTR):
        c = ex[t, 8:16, :]
        w0, w1, w2, w3, w4 = weights
        adv.append(w0 * c + w1 * east(c) + w2 * west(c) + w3 * ex[t, 9:17, :] + w4 * ex[t, 7:15, :])

    def keep_edge(t, value):
        mp[NF + 4 + t] = mprime(value)

    react(adv, rate_at, wet8, gain, keep_edge)

    def layered(row):
        return jnp.broadcast_to(row, (K, COLS))

    def from_west(row):
        return pltpu.roll(layered(row), 69, 1, stride=8, stride_axis=0)

    def from_east(row):
        return pltpu.roll(layered(row), 3, 1, stride=8, stride_axis=0)

    def lat_east(a, row):
        return jnp.where(at_last, from_east(row), east(a))

    def lat_west(a, row):
        return jnp.where(at_first, from_west(row), west(a))

    kf = sub.astype(F32)
    own_depth = depth_ref[...]

    def block(ref, i):
        return ref[pl.ds(i * K, K), :]

    class Line:
        pass

    def line(ref, misc, base, er, depth_row):
        o = Line()
        o.u, o.v, o.h, o.t, o.s = (block(ref, base + i) for i in range(5))
        o.wet = (kf < layered(ref[misc * K + depth_row:misc * K + depth_row + 1, :])).astype(F32)
        o.er = er
        return around(o)

    def around(o):
        er = o.er
        o.p = 0.3 * o.h + density(o.t, o.s)

        def e(f):
            return ex[f, er:er + 1, :]

        o.ue, o.uw = lat_east(o.u, e(FU)), lat_west(o.u, e(FU))
        o.ve, o.vw = lat_east(o.v, e(FV)), lat_west(o.v, e(FV))
        o.he, o.hw = lat_east(o.h, e(FH)), lat_west(o.h, e(FH))
        pe = 0.3 * e(FH) + density(e(FT), e(FS))
        o.pe = lat_east(o.p, pe)
        wet_e = (kf < from_east(e(FD))).astype(F32)
        wet_w = (kf < from_west(e(FD))).astype(F32)
        o.we = o.wet * jnp.where(at_last, wet_e, east(o.wet))
        o.ww = o.wet * jnp.where(at_first, wet_w, west(o.wet))
        rho = density(o.t, o.s)
        o.kap = kappa_of(o.wet, jnp.where(sub < K - 1, pltpu.roll(rho, K - 1, 0) - rho, 0.0))
        return o

    def own_line(row):
        o = Line()
        o.u, o.v, o.h = layer_rows(vel, 0, row), layer_rows(vel, K, row), layer_rows(thk, 0, row)
        o.p = 0.3 * o.h + density(layer_rows(hyd, 0, row), layer_rows(hyd, K, row))
        o.wet = (kf < layered(depth_ref[row:row + 1, :])).astype(F32)
        return o

    def height(o, n, s):
        wn, ws = o.wet * n.wet, o.wet * s.wet
        qe = o.we * o.u * 0.5 * (o.h + o.he)
        qw = o.ww * o.uw * 0.5 * (o.hw + o.h)
        qn = wn * o.v * 0.5 * (o.h + n.h)
        qs = ws * s.v * 0.5 * (s.h + o.h)
        return o.wet * (o.h - (qe - qw + qn - qs))

    def east_speed(o, n, s, cor):
        wn, ws = o.wet * n.wet, o.wet * s.wet
        return o.we * (o.u + cor * o.v - (o.pe - o.p) + 0.1 * laplace(o.u, o.ue, o.uw, n.u, s.u, o.we, o.ww, wn, ws))

    def north_speed(o, n, s, cor):
        wn, ws = o.wet * n.wet, o.wet * s.wet
        return wn * (o.v - cor * o.u - (n.p - o.p) + 0.1 * laplace(o.v, o.ve, o.vw, n.v, s.v, o.we, o.ww, wn, ws))

    sa = line(lat_s, N_FWD - 1, B_DA, 7, 7)
    sb = line(lat_s, N_FWD - 1, B_DB, 6, 6)
    sc = Line()
    sc.v, sc.h = block(lat_s, B_C), block(lat_s, B_C + 1)
    sc.wet = (kf < layered(lat_s[(N_FWD - 1) * K + 5:(N_FWD - 1) * K + 6, :])).astype(F32)
    na = line(lat_n, N_BWD - 1, B_DA, 16, 0)
    nb = line(lat_n, N_BWD - 1, B_DB, 17, 1)
    nc = Line()
    nc.h = block(lat_n, B_C)
    nc.wet = (kf < layered(lat_n[(N_BWD - 1) * K + 2:(N_BWD - 1) * K + 3, :])).astype(F32)
    row0, row7 = own_line(0), own_line(ROWS - 1)

    sa.nu = east_speed(sa, row0, sb, 0.3 * latitude(-1.0))
    sa.nv = north_speed(sa, row0, sb, 0.3 * latitude(-1.0))
    sa.nh = height(sa, row0, sb)
    sb.nv = north_speed(sb, sa, sc, 0.3 * latitude(-2.0))
    sb.nh = height(sb, sa, sc)
    na.nu = east_speed(na, nb, row7, 0.3 * latitude(float(ROWS)))
    na.nv = north_speed(na, nb, row7, 0.3 * latitude(float(ROWS)))
    na.nh = height(na, nb, row7)
    nb.nh = height(nb, nc, na)
    for i, value in enumerate((sa.nv, sa.nh, sa.kap, na.nh, na.kap)):
        lw[1 + i] = value

    lat_col = latitude(sub.astype(F32))
    cor8 = 0.3 * lat_col
    depth_mp = mp[FD]

    def row_of(ref, at):
        return jnp.broadcast_to(ref[pl.ds(at, 1), :], (ROWS, COLS))

    def around_sides(value, f, shift):
        edge_value = pltpu.roll(mp[f], shift, 1)
        return jnp.where(at_last, edge_value, east(value)), jnp.where(at_first, edge_value, west(value))

    def around_ends(value, rn, rs):
        return jnp.where(end_row, rn, pltpu.roll(value, ROWS - 1, 0)), jnp.where(top_row, rs, pltpu.roll(value, 1, 0))

    dep_e, dep_w = around_sides(own_depth, FD, 67)
    dep_n, dep_s = around_ends(own_depth, row_of(lat_n, (N_BWD - 1) * K), row_of(lat_s, (N_FWD - 1) * K + 7))

    def cells(k, over):
        shift = 67 + 8 * k
        kk = k.astype(F32)
        at = pl.ds(pl.multiple_of(k * ROWS, ROWS), ROWS)
        at2 = pl.ds(pl.multiple_of((k + K) * ROWS, ROWS), ROWS)
        u, v, h, t_, s_ = vel[at, :], vel[at2, :], thk[at, :], hyd[at, :], hyd[at2, :]
        wet = (kk < own_depth).astype(F32)
        we = wet * (kk < dep_e).astype(F32)
        ww = wet * (kk < dep_w).astype(F32)
        wn = wet * (kk < dep_n).astype(F32)
        ws = wet * (kk < dep_s).astype(F32)

        def near(value, f, i):
            e, w = around_sides(value, f, shift)
            n, s = around_ends(value, row_of(lat_n, (B_DA + i) * K + k), row_of(lat_s, (B_DA + i) * K + k))
            return e, w, n, s

        ue, uw, un, us = near(u, FU, 0)
        ve, vw, vn, vs = near(v, FV, 1)
        he, hw, hn, hs = near(h, FH, 2)
        t_e, tw, t_n, ts = near(t_, FT, 3)
        s_e, sw, s_n, ss = near(s_, FS, 4)
        p = 0.3 * h + density(t_, s_)
        pe = 0.3 * he + density(t_e, s_e)
        pn = 0.3 * hn + density(t_n, s_n)
        nu = we * (u + cor8 * v - (pe - p) + 0.1 * laplace(u, ue, uw, un, us, we, ww, wn, ws))
        nv = wn * (v - cor8 * u - (pn - p) + 0.1 * laplace(v, ve, vw, vn, vs, we, ww, wn, ws))
        qe = we * u * 0.5 * (h + he)
        qw = ww * uw * 0.5 * (hw + h)
        qn = wn * v * 0.5 * (h + hn)
        qs = ws * vs * 0.5 * (hs + h)
        nh = wet * (h - (qe - qw + qn - qs))
        out_vel[at, :] = nu
        out_vel[at2, :] = nv
        out_thk[at, :] = nh
        lower = jnp.minimum(k + 1, K - 1)
        al = pl.ds(pl.multiple_of(lower * ROWS, ROWS), ROWS)
        al2 = pl.ds(pl.multiple_of((lower + K) * ROWS, ROWS), ROWS)
        below = density(hyd[al, :], hyd[al2, :]) - density(t_, s_)
        kap = kappa_of(wet, below)
        chl = trc[pl.ds(pl.multiple_of((k + K) * ROWS, ROWS), ROWS), :]
        att = wet * (0.1 + 0.2 * chl * chl)
        light = sun8 * jnp.exp(-over)
        absorbed = light * (1.0 - jnp.exp(-att))
        out_abs[at, :] = absorbed
        out_hyd[at, :] = wet * (t_ + 0.1 * laplace(t_, t_e, tw, t_n, ts, we, ww, wn, ws)) + absorbed
        out_hyd[at2, :] = wet * (s_ + 0.1 * laplace(s_, s_e, sw, s_n, ss, we, ww, wn, ws))
        nhe = jnp.where(at_last, pltpu.roll(mp[FD + 1], shift, 1), east(nh))
        kape = jnp.where(at_last, pltpu.roll(mp[FD + 2], shift, 1), east(kap))
        nhn = jnp.where(end_row, row_of(lw.at[4], k), pltpu.roll(nh, ROWS - 1, 0))
        kapn = jnp.where(end_row, row_of(lw.at[5], k), pltpu.roll(kap, ROWS - 1, 0))
        te = nu * 0.5 * (nh + nhe)
        de = we * 0.5 * (kap + kape)
        tn = nv * 0.5 * (nh + nhn)
        dn = wn * 0.5 * (kap + kapn)
        tw = jnp.where(at_first, pltpu.roll(mp[FD + 3], shift, 1), west(te))
        dw = jnp.where(at_first, pltpu.roll(mp[FD + 4], shift, 1), west(de))
        ts = jnp.where(top_row, row_of(lw.at[1], k) * 0.5 * (row_of(lw.at[2], k) + nh), pltpu.roll(tn, 1, 0))
        ds = jnp.where(top_row, ws * 0.5 * (row_of(lw.at[3], k) + kap), pltpu.roll(dn, 1, 0))
        for i, w in enumerate(step_weights(te, de, tw, dw, tn, dn, ts, ds)):
            cf[i, at, :] = w
        cf[5, at, :] = SUB * grow8 * light
        cf[6, at, :] = tn
        cf[7, at, :] = dn
        return over + att

    lax.fori_loop(0, K, cells, jnp.zeros((ROWS, COLS), F32))

    leaving = [
        pltpu.make_async_copy(src, dst, sems.at[i])
        for i, (src, dst) in enumerate(((out_vel, to_vel), (out_thk, to_thk), (out_hyd, to_hyd), (out_abs, to_abs)))
    ]
    for move in leaving:
        move.start()

    def outer(o, te_row, grow, lat_row, tn, dn, ts, ds, near_ref, north_of, south_of, er, kept):
        he = lat_east(o.nh, es[0, er:er + 1, :])
        kape = lat_east(o.kap, es[1, er:er + 1, :])
        te = o.nu * 0.5 * (o.nh + he)
        de = o.we * 0.5 * (o.kap + kape)
        tw = lat_west(te, es[2, er:er + 1, :])
        dw = lat_west(de, es[3, er:er + 1, :])
        w0, w1, w2, w3, w4 = step_weights(te, de, tw, dw, tn, dn, ts, ds)
        chl = block(near_ref, B_A + 1)
        att = o.wet * (0.1 + 0.2 * chl * chl)
        total = att
        for shift in (1, 2, 4):
            total = total + jnp.where(sub >= shift, pltpu.roll(total, shift, 0), 0.0)
        lat_here = latitude(lat_row)
        gain = SUB * layered(grow) * ((1.0 - 0.8 * lat_here * lat_here) * jnp.exp(-(total - att)))
        adv = []
        for t in range(NTR):
            c = block(near_ref, B_A + t)
            row = ex[t, er:er + 1, :]
            adv.append(w0 * c + w1 * lat_east(c, row) + w2 * lat_west(c, row) + w3 * north_of(t) + w4 * south_of(t))

        def keep(t, value):
            kept[pl.ds(t * K, K), :] = value

        react(adv, rate_at, o.wet, gain, keep)

    h0 = layer_rows(out_thk, 0, 0)
    kap0 = kappa_of(row0.wet, row_below(hyd, 0, sub))
    wn_s = sa.wet * row0.wet
    outer(sa, None, lat_s[(N_FWD - 1) * K + 3:(N_FWD - 1) * K + 4, :], -1.0,
          sa.nv * 0.5 * (sa.nh + h0), wn_s * 0.5 * (sa.kap + kap0),
          sb.nv * 0.5 * (sb.nh + sa.nh), sb.wet * sa.wet * 0.5 * (sb.kap + sa.kap),
          lat_s, lambda t: layer_rows(trc, t * K, 0), lambda t: block(lat_s, B_B + t), 7, l1s)
    outer(na, None, lat_n[(N_BWD - 1) * K + 3:(N_BWD - 1) * K + 4, :], float(ROWS),
          na.nv * 0.5 * (na.nh + nb.nh), na.wet * nb.wet * 0.5 * (na.kap + nb.kap),
          layer_rows(cf.at[6], 0, ROWS - 1), layer_rows(cf.at[7], 0, ROWS - 1),
          lat_n, lambda t: block(lat_n, B_B + t), lambda t: layer_rows(trc, t * K, ROWS - 1), 16, l1n)

    def substep(src, mp_base, end_n, end_s, put, after):
        def advect(k):
            shift = 67 + 8 * k
            at = pl.ds(pl.multiple_of(k * ROWS, ROWS), ROWS)
            w0, w1, w2, w3, w4 = (cf[i, at, :] for i in range(5))
            adv = []
            for t in range(NTR):
                c = src[pl.ds(pl.multiple_of((t * K + k) * ROWS, ROWS), ROWS), :]
                e, w = around_sides(c, mp_base + t, shift)
                n, s = around_ends(c, row_of(end_n, t * K + k), row_of(end_s, t * K + k))
                adv.append(w0 * c + w1 * e + w2 * w + w3 * n + w4 * s)
            return adv, (k.astype(F32) < own_depth).astype(F32), cf[5, at, :]

        def body(j, carry):
            ks = [GROUP * j + i for i in range(GROUP)]
            cells, wets, gains = zip(*(advect(k) for k in ks))

            def keep(i, t, value):
                put(t, ks[i], value)

            react_all(cells, rate_at, wets, gains, keep)
            after(j)
            return carry

        lax.fori_loop(0, K // GROUP, body, 0)

    def put_first(t, k, value):
        c1[pl.ds(pl.multiple_of((t * K + k) * ROWS, ROWS), ROWS), :] = value

    def put_last(t, k, value):
        out_trc[t, k] = value

    def leave(j):
        layers = pl.ds(GROUP * j, GROUP)
        return pltpu.make_async_copy(out_trc.at[:, layers], to_trc.at[:, layers], sems.at[4 + j])

    substep(trc, 0, lat_n, lat_s, put_first, lambda j: None)
    substep(c1, NF + 4, l1n, l1s, put_last, lambda j: leave(j).start())
    for move in leaving:
        move.wait()
    for j in range(K // GROUP):
        leave(j).wait()


def row_below(hyd, row, sub):
    rho = density(layer_rows(hyd, 0, row), layer_rows(hyd, K, row))
    return jnp.where(sub < K - 1, pltpu.roll(rho, K - 1, 0) - rho, 0.0)


def rate_table(after, rr, out):
    for t in range(NTR):
        for s in range(NTR):
            out[pl.ds((t * NTR + s) * ROWS, ROWS), :] = jnp.full((ROWS, COLS), SUB * rr[t, s])


def near(*dims):
    return pltpu.VMEM(dims, F32)


def far(*dims):
    return jax.ShapeDtypeStruct(dims, F32)


def held(x):
    return pltpu.with_memory_space_constraint(x, pltpu.VMEM)


def call(kernel, out_shape, spaces, scratch=(), flops=100000, out="v"):
    spec = {"a": pl.BlockSpec(memory_space=pl.ANY), "v": pl.BlockSpec(memory_space=pltpu.VMEM), "s": pl.BlockSpec(memory_space=pltpu.SMEM)}
    return pl.pallas_call(
        kernel,
        out_shape=out_shape,
        in_specs=[spec[c] for c in spaces],
        out_specs=tuple(spec[out] for _ in out_shape),
        scratch_shapes=list(scratch),
        cost_estimate=pl.CostEstimate(flops=flops, bytes_accessed=100000, transcendentals=0),
    )


def per_device(velocity, thickness, hydrography, tracers, land_mask, bottom_layer, row_biome, reaction_rates, growth_rates):
    lat, lon = lax.axis_size("lat"), lax.axis_size("lon")
    vel = velocity.reshape(2 * K * ROWS, COLS)
    thk = thickness.reshape(K * ROWS, COLS)
    hyd = hydrography.reshape(2 * K * ROWS, COLS)
    trc = tracers.reshape(NTR * K * ROWS, COLS)

    def swap(n, start):
        return [p for i in range(start, n - 1, 2) for p in ((i, i + 1), (i + 1, i))]

    *state, own = (held(x) for x in call(
        lon_pack,
        (near(2 * K * ROWS, COLS), near(K * ROWS, COLS), near(2 * K * ROWS, COLS), near(NTR * K * ROWS, COLS),
         near(ROWS, COLS), near(ROWS, COLS), near(PAIRS * ROWS, COLS)),
        "vvvvvvss",
    )(vel, thk, hyd, trc, land_mask, bottom_layer, row_biome, growth_rates))
    outer = held(lax.ppermute(own, "lon", swap(lon, 1)))
    inner = held(lax.ppermute(own, "lon", swap(lon, 0)))
    fwd, bwd = call(lat_pack, (near(C_FWD, COLS), near(C_BWD, COLS)), "vvvvvvv")(
        *state, own)
    edge, fwd, bwd = call(
        edge_pack, (near(NF * ROWS, COLS), near(ROWS_FWD, COLS), near(ROWS_BWD, COLS)), "vvvvv"
    )(own, inner, outer, held(fwd), held(bwd))
    edge = held(edge)
    table = held(call(rate_table, (near(NTR * NTR * ROWS, COLS),), "vs")(edge, reaction_rates)[0])
    lat_s = held(lax.ppermute(fwd, "lat", [(i, i + 1) for i in range(lat - 1)]))
    lat_n = held(lax.ppermute(bwd, "lat", [(i + 1, i) for i in range(lat - 1)]))

    def body(*refs):
        step(lat * ROWS, *refs)

    outs = call(
        body,
        (far(2 * K * ROWS, COLS), far(K * ROWS, COLS), far(2 * K * ROWS, COLS), far(NTR, K, ROWS, COLS), far(K * ROWS, COLS)),
        "vvvvvvvvvv",
        out="a",
        scratch=[
            pltpu.VMEM((NF, 24, COLS), F32),
            pltpu.VMEM((4, 24, COLS), F32),
            pltpu.VMEM((NF + 4 + NTR, ROWS, COLS), F32),
            pltpu.VMEM((NTR * K, COLS), F32),
            pltpu.VMEM((NTR * K, COLS), F32),
            pltpu.VMEM((6, ROWS, COLS), F32),
            pltpu.VMEM((NTR * K * ROWS, COLS), F32),
            pltpu.VMEM((8, K * ROWS, COLS), F32),
            pltpu.VMEM((2 * K * ROWS, COLS), F32),
            pltpu.VMEM((K * ROWS, COLS), F32),
            pltpu.VMEM((2 * K * ROWS, COLS), F32),
            pltpu.VMEM((NTR, K, ROWS, COLS), F32),
            pltpu.VMEM((K * ROWS, COLS), F32),
            pltpu.SemaphoreType.DMA((4 + K // GROUP,)),
        ],
    )(*state, table, lat_s, lat_n, edge)
    new_vel, new_thk, new_hyd, new_trc, absorbed = outs
    return (new_vel.reshape(velocity.shape), new_thk.reshape(thickness.shape), new_hyd.reshape(hydrography.shape),
            new_trc.reshape(tracers.shape), absorbed.reshape(thickness.shape))


def solution(mesh):
    field = P(None, "lat", "lon")
    fields = P(None, None, "lat", "lon")
    in_specs = (fields, field, fields, fields, P("lat", "lon"), P("lat", "lon"), P("lat"), P(), P())
    out_specs = (fields, field, fields, fields, field)
    return jax.shard_map(per_device, mesh=mesh, in_specs=in_specs, out_specs=out_specs, check_vma=False)
```

```python
import jax
import jax.numpy as jnp
from jax import lax
from jax.experimental import pallas as pl
from jax.experimental.pallas import tpu as pltpu
from jax.sharding import PartitionSpec as P

F32 = jnp.float32
NSUB = 2
SUB = 1.0 / NSUB
NTR = 17
K = 8
ROWS = 8
COLS = 128
FU, FV, FH, FT, FS, FD = 17, 18, 19, 20, 21, 22
NF = 24
GROUP = 2
PAIRS = NF // 2
B_A, B_B, B_DA, B_DB, B_C = 0, 17, 34, 39, 44
N_FWD, N_BWD = 46, 45
C_FWD, C_BWD = N_FWD * K, N_BWD * K
ROWS_FWD, ROWS_BWD = C_FWD + 24, C_BWD + 24


def lanes(shape):
    return lax.broadcasted_iota(jnp.int32, shape, len(shape) - 1)


def subs(shape):
    return lax.broadcasted_iota(jnp.int32, shape, len(shape) - 2)


def growth_of(biome_ref, rates_ref, row):
    kind = biome_ref[row]
    rate = rates_ref[0]
    for i in range(1, rates_ref.shape[0]):
        rate = jnp.where(kind == i, rates_ref[i], rate)
    return rate


def layer_rows(ref, plane, row):
    return ref[pl.ds(plane * ROWS + row, K, stride=ROWS), :]


def lat_pack(vel, thk, hyd, trc, after, fwd, bwd):
    def put(out, block, value):
        out[pl.ds(block * K, K), :] = value

    def state(out, block, row):
        put(out, block, layer_rows(vel, 0, row))
        put(out, block + 1, layer_rows(vel, K, row))
        put(out, block + 2, layer_rows(thk, 0, row))
        put(out, block + 3, layer_rows(hyd, 0, row))
        put(out, block + 4, layer_rows(hyd, K, row))

    for out, a, b in ((fwd, ROWS - 1, ROWS - 2), (bwd, 0, 1)):
        for t in range(NTR):
            put(out, B_A + t, layer_rows(trc, t * K, a))
            put(out, B_B + t, layer_rows(trc, t * K, b))
        state(out, B_DA, a)
        state(out, B_DB, b)
    put(fwd, B_C, layer_rows(vel, K, ROWS - 3))
    put(fwd, B_C + 1, layer_rows(thk, 0, ROWS - 3))
    put(bwd, B_C, layer_rows(thk, 0, 2))


def lon_pack(vel_in, thk_in, hyd_in, trc_in, land, bottom, biome, rates, vel, thk, hyd, trc, depth_out, grow, out):
    for src, dst in ((trc_in, trc), (vel_in, vel), (hyd_in, hyd), (thk_in, thk)):
        dst[...] = src[...]
    depth = (land[...] * bottom[...]).astype(F32)
    depth_out[...] = depth
    sub = subs((ROWS, COLS))
    grow_tile = jnp.zeros((ROWS, COLS), F32)
    for r in range(ROWS):
        grow_tile = jnp.where(sub == r, growth_of(biome, rates, r), grow_tile)
    grow[...] = grow_tile
    group = lanes((ROWS, COLS)) >> 3

    def plane(f, k):
        if f < NTR:
            return trc_in[pl.ds((f * K + k) * ROWS, ROWS), :]
        if f < FH:
            return vel_in[pl.ds(((f - FU) * K + k) * ROWS, ROWS), :]
        if f == FH:
            return thk_in[pl.ds(k * ROWS, ROWS), :]
        if f < FD:
            return hyd_in[pl.ds(((f - FT) * K + k) * ROWS, ROWS), :]
        return depth

    for p in range(PAIRS):
        packed = jnp.zeros((ROWS, COLS), F32)
        for half in range(2):
            f = p + PAIRS * half
            if f > FD:
                continue
            for k in range(K):
                moved = pltpu.roll(plane(f, k), (half * 64 + (7 - k) * 8 + 4) % COLS, 1)
                packed = jnp.where(group == half * 8 + 7 - k, moved, packed)
        out[pl.ds(p * ROWS, ROWS), :] = packed


def edge_pack(own, inner, outer, depth_ref, grow, fwd_in, bwd_in, edge, fwd, bwd):
    lane = lanes((ROWS, COLS))
    low = (lane & 7) < 4
    left = lane < 64
    odd = jnp.full((ROWS, COLS), lax.axis_index("lon") & 1) == 1
    for p in range(PAIRS):
        at = pl.ds(p * ROWS, ROWS)
        o, a, b = own[at, :], inner[at, :], outer[at, :]
        x = jnp.where(low, jnp.where(odd, a, b), o)
        y = jnp.where(low, o, jnp.where(odd, b, a))
        edge[pl.ds(p * ROWS, ROWS), :] = jnp.where(left, x, pltpu.roll(y, 64, 1))
        edge[pl.ds((p + PAIRS) * ROWS, ROWS), :] = jnp.where(left, pltpu.roll(x, 64, 1), y)
    place = lane & 7
    corners = []
    for i in range(3):
        packed = jnp.zeros((ROWS, COLS), F32)
        for q in range(min(7, NTR - 7 * i)):
            moved = pltpu.roll(edge[pl.ds((7 * i + q) * ROWS, ROWS), :], (q - 3) % COLS, 1)
            packed = jnp.where(place == jnp.where(left, q, q + 1), moved, packed)
        if i == 2:
            packed = jnp.where(place == 6, grow[...], packed)
        corners.append(packed)
    for out, source, at, a, b, c in ((fwd, fwd_in, C_FWD, 7, 6, 5), (bwd, bwd_in, C_BWD, 0, 1, 2)):
        out[pl.ds(0, at), :] = source[...]
        for i, row in enumerate((a, b, c)):
            out[pl.ds(at + i * 8, 8), :] = edge[pl.ds(128 + row, 8, stride=8), :]
            out[pl.ds(at + i * 8, 1), :] = corners[i][a:a + 1, :]
            out[pl.ds(at + i * 8 + 7, 1), :] = depth_ref[row:row + 1, :]


def kappa_of(wet, below):
    return wet * (0.02 + 0.1 / (1.0 + 10.0 * below * below))


def density(t, s):
    return 0.25 * s - 0.2 * t


def laplace(a, ae, aw, an, as_, we, ww, wn, ws):
    return we * (ae - a) - ww * (a - aw) + wn * (an - a) - ws * (a - as_)


def parts(transport, diffuse):
    return jnp.maximum(transport, 0.0) + diffuse, jnp.minimum(transport, 0.0) - diffuse


def step_weights(te, de, tw, dw, tn, dn, ts, ds):
    ae, be = parts(te, de)
    aw, bw = parts(tw, dw)
    an, bn = parts(tn, dn)
    as_, bs = parts(ts, ds)
    return 1.0 - SUB * (ae - bw + an - bs), -SUB * be, SUB * aw, -SUB * bn, SUB * as_


def react(adv, rate_at, wet, gain, store):
    react_all([adv], rate_at, [wet], [gain], lambda i, t, value: store(t, value))


def react_all(cells, rate_at, wets, gains, store):
    uptakes = []
    for adv, gain in zip(cells, gains):
        square = adv[0] * adv[0]
        uptakes.append(gain * adv[1] * square / (1.0 + square))
    for t in range(NTR):
        totals = [adv[t] for adv in cells]
        for s in range(NTR):
            rate = rate_at(t, s)
            totals = [total + rate * adv[s] for total, adv in zip(totals, cells)]
        for i, total in enumerate(totals):
            if t == 0:
                total = total - uptakes[i]
            if t == 1:
                total = total + uptakes[i]
            store(i, t, wets[i] * total)


def step(total_rows, vel, thk, hyd, trc, depth_ref, grow, table, lat_s, lat_n, edge,
         to_vel, to_thk, to_hyd, to_trc, to_abs,
         ex, es, mp, l1s, l1n, lw, c1, cf, out_vel, out_thk, out_hyd, out_trc, out_abs, sems):
    first = (lax.axis_index("lat") * ROWS).astype(F32)

    def latitude(row):
        return 2.0 * (first + row + 0.5) / total_rows - 1.0

    def rate_at(t, s):
        return table[pl.ds((t * NTR + s) * ROWS, ROWS), :]

    lane = lanes((ROWS, COLS))
    sub = subs((ROWS, COLS))
    at_first, at_last = lane == 0, lane == COLS - 1
    top_row, end_row = sub == 0, sub == ROWS - 1

    def mprime(value):
        return jnp.where((lane & 7) == 5, pltpu.roll(value, 2, 1), pltpu.roll(value, 64, 1))

    cor_s = lat_s.at[pl.ds(C_FWD, 24), :]
    cor_n = lat_n.at[pl.ds(C_BWD, 24), :]

    for f in range(NF - 1):
        own = edge[pl.ds(f * ROWS, ROWS), :]
        mp[f] = mprime(own)
        if f >= NTR:
            ex[f, 0:8, :] = jnp.zeros((8, COLS), F32)
            ex[f, 16:24, :] = jnp.zeros((8, COLS), F32)
            for i in range(3):
                at = i * 8 + f - 16
                ex[f, 7 - i:8 - i, :] = cor_s[at:at + 1, :]
                ex[f, 16 + i:17 + i, :] = cor_n[at:at + 1, :]
        else:
            for ref, at in ((cor_s, 7), (cor_n, 16)):
                row = jnp.broadcast_to(ref[f // 7 * 8:f // 7 * 8 + 1, :], (ROWS, COLS))
                ex[f, at:at + 1, :] = pltpu.roll(row, (3 - f % 7) % COLS, 1)[0:1, :]
        ex[f, 8:16, :] = own

    def east(a):
        return pltpu.roll(a, COLS - 1, 1)

    def west(a):
        return pltpu.roll(a, 1, 1)

    def north(a):
        return pltpu.roll(a, 23, 0)

    def south(a):
        return pltpu.roll(a, 1, 0)

    big = (24, COLS)
    layer = 7 - ((lanes(big) >> 3) & 7)
    u, v, h, t_, s_ = ex[FU], ex[FV], ex[FH], ex[FT], ex[FS]
    wet = (layer.astype(F32) < ex[FD]).astype(F32)
    rho = density(t_, s_)
    p = 0.3 * h + rho
    cor = 0.3 * latitude((subs(big) - 8).astype(F32))
    we = wet * east(wet)
    wn = wet * north(wet)
    ww, ws = west(we), south(wn)
    lap_u = laplace(u, east(u), west(u), north(u), south(u), we, ww, wn, ws)
    lap_v = laplace(v, east(v), west(v), north(v), south(v), we, ww, wn, ws)
    new_u = we * (u + cor * v - (east(p) - p) + 0.1 * lap_u)
    new_v = wn * (v - cor * u - (north(p) - p) + 0.1 * lap_v)
    qe = we * u * 0.5 * (h + east(h))
    qn = wn * v * 0.5 * (h + north(h))
    new_h = wet * (h - (qe - west(qe) + qn - south(qn)))
    kap = kappa_of(wet, jnp.where(layer < K - 1, pltpu.roll(rho, 8, 1) - rho, 0.0))
    te = new_u * 0.5 * (new_h + east(new_h))
    tn = new_v * 0.5 * (new_h + north(new_h))
    de = we * 0.5 * (kap + east(kap))
    dn = wn * 0.5 * (kap + north(kap))
    for i, value in enumerate((new_h, kap, te, de)):
        es[i] = value
        mp[FD + 1 + i] = mprime(value[8:16])
    weights = step_weights(te, de, west(te), west(de), tn, dn, south(tn), south(dn))
    weights = [w[8:16] for w in weights]
    small_layer = 7 - ((lane >> 3) & 7)
    wet8 = wet[8:16]
    chl = ex[1, 8:16, :]
    att = wet8 * (0.1 + 0.2 * chl * chl)
    total = att
    for shift in (1, 2, 4):
        total = total + jnp.where(small_layer >= shift, pltpu.roll(total, COLS - 8 * shift, 1), 0.0)
    lat8 = latitude(sub.astype(F32))
    sun8 = 1.0 - 0.8 * lat8 * lat8
    grow8 = grow[...]
    gain = SUB * grow8 * sun8 * jnp.exp(-(total - att))
    adv = []
    for t in range(NTR):
        c = ex[t, 8:16, :]
        w0, w1, w2, w3, w4 = weights
        adv.append(w0 * c + w1 * east(c) + w2 * west(c) + w3 * ex[t, 9:17, :] + w4 * ex[t, 7:15, :])

    def keep_edge(t, value):
        mp[NF + 4 + t] = mprime(value)

    react(adv, rate_at, wet8, gain, keep_edge)

    def layered(row):
        return jnp.broadcast_to(row, (K, COLS))

    def from_west(row):
        return pltpu.roll(layered(row), 69, 1, stride=8, stride_axis=0)

    def from_east(row):
        return pltpu.roll(layered(row), 3, 1, stride=8, stride_axis=0)

    def lat_east(a, row):
        return jnp.where(at_last, from_east(row), east(a))

    def lat_west(a, row):
        return jnp.where(at_first, from_west(row), west(a))

    kf = sub.astype(F32)
    own_depth = depth_ref[...]

    def block(ref, i):
        return ref[pl.ds(i * K, K), :]

    class Line:
        pass

    def line(ref, base, er, depth_row):
        o = Line()
        o.u, o.v, o.h, o.t, o.s = (block(ref, base + i) for i in range(5))
        o.wet = (kf < layered(depth_row)).astype(F32)
        o.er = er
        return around(o)

    def around(o):
        er = o.er
        o.p = 0.3 * o.h + density(o.t, o.s)

        def e(f):
            return ex[f, er:er + 1, :]

        o.ue, o.uw = lat_east(o.u, e(FU)), lat_west(o.u, e(FU))
        o.ve, o.vw = lat_east(o.v, e(FV)), lat_west(o.v, e(FV))
        o.he, o.hw = lat_east(o.h, e(FH)), lat_west(o.h, e(FH))
        pe = 0.3 * e(FH) + density(e(FT), e(FS))
        o.pe = lat_east(o.p, pe)
        wet_e = (kf < from_east(e(FD))).astype(F32)
        wet_w = (kf < from_west(e(FD))).astype(F32)
        o.we = o.wet * jnp.where(at_last, wet_e, east(o.wet))
        o.ww = o.wet * jnp.where(at_first, wet_w, west(o.wet))
        rho = density(o.t, o.s)
        o.kap = kappa_of(o.wet, jnp.where(sub < K - 1, pltpu.roll(rho, K - 1, 0) - rho, 0.0))
        return o

    def own_line(row):
        o = Line()
        o.u, o.v, o.h = layer_rows(vel, 0, row), layer_rows(vel, K, row), layer_rows(thk, 0, row)
        o.p = 0.3 * o.h + density(layer_rows(hyd, 0, row), layer_rows(hyd, K, row))
        o.wet = (kf < layered(depth_ref[row:row + 1, :])).astype(F32)
        return o

    def height(o, n, s):
        wn, ws = o.wet * n.wet, o.wet * s.wet
        qe = o.we * o.u * 0.5 * (o.h + o.he)
        qw = o.ww * o.uw * 0.5 * (o.hw + o.h)
        qn = wn * o.v * 0.5 * (o.h + n.h)
        qs = ws * s.v * 0.5 * (s.h + o.h)
        return o.wet * (o.h - (qe - qw + qn - qs))

    def east_speed(o, n, s, cor):
        wn, ws = o.wet * n.wet, o.wet * s.wet
        return o.we * (o.u + cor * o.v - (o.pe - o.p) + 0.1 * laplace(o.u, o.ue, o.uw, n.u, s.u, o.we, o.ww, wn, ws))

    def north_speed(o, n, s, cor):
        wn, ws = o.wet * n.wet, o.wet * s.wet
        return wn * (o.v - cor * o.u - (n.p - o.p) + 0.1 * laplace(o.v, o.ve, o.vw, n.v, s.v, o.we, o.ww, wn, ws))

    depths_s = [cor_s[i * 8 + 7:i * 8 + 8, :] for i in range(3)]
    depths_n = [cor_n[i * 8 + 7:i * 8 + 8, :] for i in range(3)]
    sa = line(lat_s, B_DA, 7, depths_s[0])
    sb = line(lat_s, B_DB, 6, depths_s[1])
    sc = Line()
    sc.v, sc.h = block(lat_s, B_C), block(lat_s, B_C + 1)
    sc.wet = (kf < layered(depths_s[2])).astype(F32)
    na = line(lat_n, B_DA, 16, depths_n[0])
    nb = line(lat_n, B_DB, 17, depths_n[1])
    nc = Line()
    nc.h = block(lat_n, B_C)
    nc.wet = (kf < layered(depths_n[2])).astype(F32)
    row0, row7 = own_line(0), own_line(ROWS - 1)

    sa.nu = east_speed(sa, row0, sb, 0.3 * latitude(-1.0))
    sa.nv = north_speed(sa, row0, sb, 0.3 * latitude(-1.0))
    sa.nh = height(sa, row0, sb)
    sb.nv = north_speed(sb, sa, sc, 0.3 * latitude(-2.0))
    sb.nh = height(sb, sa, sc)
    na.nu = east_speed(na, nb, row7, 0.3 * latitude(float(ROWS)))
    na.nv = north_speed(na, nb, row7, 0.3 * latitude(float(ROWS)))
    na.nh = height(na, nb, row7)
    nb.nh = height(nb, nc, na)
    for i, value in enumerate((sa.nv, sa.nh, sa.kap, na.nh, na.kap)):
        lw[1 + i] = value

    lat_col = latitude(sub.astype(F32))
    cor8 = 0.3 * lat_col
    depth_mp = mp[FD]

    def row_of(ref, at):
        return jnp.broadcast_to(ref[pl.ds(at, 1), :], (ROWS, COLS))

    def around_sides(value, f, shift):
        edge_value = pltpu.roll(mp[f], shift, 1)
        return jnp.where(at_last, edge_value, east(value)), jnp.where(at_first, edge_value, west(value))

    def around_ends(value, rn, rs):
        return jnp.where(end_row, rn, pltpu.roll(value, ROWS - 1, 0)), jnp.where(top_row, rs, pltpu.roll(value, 1, 0))

    dep_e, dep_w = around_sides(own_depth, FD, 67)
    dep_n, dep_s = around_ends(own_depth, row_of(cor_n, 7), row_of(cor_s, 7))

    def cells(k, over):
        shift = 67 + 8 * k
        kk = k.astype(F32)
        at = pl.ds(pl.multiple_of(k * ROWS, ROWS), ROWS)
        at2 = pl.ds(pl.multiple_of((k + K) * ROWS, ROWS), ROWS)
        u, v, h, t_, s_ = vel[at, :], vel[at2, :], thk[at, :], hyd[at, :], hyd[at2, :]
        wet = (kk < own_depth).astype(F32)
        we = wet * (kk < dep_e).astype(F32)
        ww = wet * (kk < dep_w).astype(F32)
        wn = wet * (kk < dep_n).astype(F32)
        ws = wet * (kk < dep_s).astype(F32)

        def near(value, f, i):
            e, w = around_sides(value, f, shift)
            n, s = around_ends(value, row_of(lat_n, (B_DA + i) * K + k), row_of(lat_s, (B_DA + i) * K + k))
            return e, w, n, s

        ue, uw, un, us = near(u, FU, 0)
        ve, vw, vn, vs = near(v, FV, 1)
        he, hw, hn, hs = near(h, FH, 2)
        t_e, tw, t_n, ts = near(t_, FT, 3)
        s_e, sw, s_n, ss = near(s_, FS, 4)
        p = 0.3 * h + density(t_, s_)
        pe = 0.3 * he + density(t_e, s_e)
        pn = 0.3 * hn + density(t_n, s_n)
        nu = we * (u + cor8 * v - (pe - p) + 0.1 * laplace(u, ue, uw, un, us, we, ww, wn, ws))
        nv = wn * (v - cor8 * u - (pn - p) + 0.1 * laplace(v, ve, vw, vn, vs, we, ww, wn, ws))
        qe = we * u * 0.5 * (h + he)
        qw = ww * uw * 0.5 * (hw + h)
        qn = wn * v * 0.5 * (h + hn)
        qs = ws * vs * 0.5 * (hs + h)
        nh = wet * (h - (qe - qw + qn - qs))
        out_vel[at, :] = nu
        out_vel[at2, :] = nv
        out_thk[at, :] = nh
        lower = jnp.minimum(k + 1, K - 1)
        al = pl.ds(pl.multiple_of(lower * ROWS, ROWS), ROWS)
        al2 = pl.ds(pl.multiple_of((lower + K) * ROWS, ROWS), ROWS)
        below = density(hyd[al, :], hyd[al2, :]) - density(t_, s_)
        kap = kappa_of(wet, below)
        chl = trc[pl.ds(pl.multiple_of((k + K) * ROWS, ROWS), ROWS), :]
        att = wet * (0.1 + 0.2 * chl * chl)
        light = sun8 * jnp.exp(-over)
        absorbed = light * (1.0 - jnp.exp(-att))
        out_abs[at, :] = absorbed
        out_hyd[at, :] = wet * (t_ + 0.1 * laplace(t_, t_e, tw, t_n, ts, we, ww, wn, ws)) + absorbed
        out_hyd[at2, :] = wet * (s_ + 0.1 * laplace(s_, s_e, sw, s_n, ss, we, ww, wn, ws))
        nhe = jnp.where(at_last, pltpu.roll(mp[FD + 1], shift, 1), east(nh))
        kape = jnp.where(at_last, pltpu.roll(mp[FD + 2], shift, 1), east(kap))
        nhn = jnp.where(end_row, row_of(lw.at[4], k), pltpu.roll(nh, ROWS - 1, 0))
        kapn = jnp.where(end_row, row_of(lw.at[5], k), pltpu.roll(kap, ROWS - 1, 0))
        te = nu * 0.5 * (nh + nhe)
        de = we * 0.5 * (kap + kape)
        tn = nv * 0.5 * (nh + nhn)
        dn = wn * 0.5 * (kap + kapn)
        tw = jnp.where(at_first, pltpu.roll(mp[FD + 3], shift, 1), west(te))
        dw = jnp.where(at_first, pltpu.roll(mp[FD + 4], shift, 1), west(de))
        ts = jnp.where(top_row, row_of(lw.at[1], k) * 0.5 * (row_of(lw.at[2], k) + nh), pltpu.roll(tn, 1, 0))
        ds = jnp.where(top_row, ws * 0.5 * (row_of(lw.at[3], k) + kap), pltpu.roll(dn, 1, 0))
        for i, w in enumerate(step_weights(te, de, tw, dw, tn, dn, ts, ds)):
            cf[i, at, :] = w
        cf[5, at, :] = SUB * grow8 * light
        cf[6, at, :] = tn
        cf[7, at, :] = dn
        return over + att

    lax.fori_loop(0, K, cells, jnp.zeros((ROWS, COLS), F32))

    leaving = [
        pltpu.make_async_copy(src, dst, sems.at[i])
        for i, (src, dst) in enumerate(((out_vel, to_vel), (out_thk, to_thk), (out_hyd, to_hyd), (out_abs, to_abs)))
    ]
    for move in leaving:
        move.start()

    def outer(o, grow, lat_row, tn, dn, ts, ds, near_ref, north_of, south_of, er):
        he = lat_east(o.nh, es[0, er:er + 1, :])
        kape = lat_east(o.kap, es[1, er:er + 1, :])
        te = o.nu * 0.5 * (o.nh + he)
        de = o.we * 0.5 * (o.kap + kape)
        tw = lat_west(te, es[2, er:er + 1, :])
        dw = lat_west(de, es[3, er:er + 1, :])
        w0, w1, w2, w3, w4 = step_weights(te, de, tw, dw, tn, dn, ts, ds)
        chl = block(near_ref, B_A + 1)
        att = o.wet * (0.1 + 0.2 * chl * chl)
        total = att
        for shift in (1, 2, 4):
            total = total + jnp.where(sub >= shift, pltpu.roll(total, shift, 0), 0.0)
        lat_here = latitude(lat_row)
        gain = SUB * layered(grow) * ((1.0 - 0.8 * lat_here * lat_here) * jnp.exp(-(total - att)))
        adv = []
        for t in range(NTR):
            c = block(near_ref, B_A + t)
            row = ex[t, er:er + 1, :]
            adv.append(w0 * c + w1 * lat_east(c, row) + w2 * lat_west(c, row) + w3 * north_of(t) + w4 * south_of(t))

        return adv, o.wet, gain

    h0 = layer_rows(out_thk, 0, 0)
    kap0 = kappa_of(row0.wet, row_below(hyd, 0, sub))
    wn_s = sa.wet * row0.wet
    lines = [outer(sa, cor_s[16:17, 6:7], -1.0,
          sa.nv * 0.5 * (sa.nh + h0), wn_s * 0.5 * (sa.kap + kap0),
          sb.nv * 0.5 * (sb.nh + sa.nh), sb.wet * sa.wet * 0.5 * (sb.kap + sa.kap),
          lat_s, lambda t: layer_rows(trc, t * K, 0), lambda t: block(lat_s, B_B + t), 7)]
    lines.append(outer(na, cor_n[16:17, 6:7], float(ROWS),
          na.nv * 0.5 * (na.nh + nb.nh), na.wet * nb.wet * 0.5 * (na.kap + nb.kap),
          layer_rows(cf.at[6], 0, ROWS - 1), layer_rows(cf.at[7], 0, ROWS - 1),
          lat_n, lambda t: block(lat_n, B_B + t), lambda t: layer_rows(trc, t * K, ROWS - 1), 16))

    def keep_line(i, t, value):
        (l1s, l1n)[i][pl.ds(t * K, K), :] = value

    react_all([o[0] for o in lines], rate_at, [o[1] for o in lines], [o[2] for o in lines], keep_line)

    def substep(src, mp_base, end_n, end_s, put, after):
        def advect(k):
            shift = 67 + 8 * k
            at = pl.ds(pl.multiple_of(k * ROWS, ROWS), ROWS)
            w0, w1, w2, w3, w4 = (cf[i, at, :] for i in range(5))
            adv = []
            for t in range(NTR):
                c = src[pl.ds(pl.multiple_of((t * K + k) * ROWS, ROWS), ROWS), :]
                e, w = around_sides(c, mp_base + t, shift)
                n, s = around_ends(c, row_of(end_n, t * K + k), row_of(end_s, t * K + k))
                adv.append(w0 * c + w1 * e + w2 * w + w3 * n + w4 * s)
            return adv, (k.astype(F32) < own_depth).astype(F32), cf[5, at, :]

        def body(j, carry):
            ks = [GROUP * j + i for i in range(GROUP)]
            cells, wets, gains = zip(*(advect(k) for k in ks))

            def keep(i, t, value):
                put(t, ks[i], value)

            react_all(cells, rate_at, wets, gains, keep)
            after(j)
            return carry

        lax.fori_loop(0, K // GROUP, body, 0)

    def put_first(t, k, value):
        c1[pl.ds(pl.multiple_of((t * K + k) * ROWS, ROWS), ROWS), :] = value

    def put_last(t, k, value):
        out_trc[t, k] = value

    def leave(j):
        layers = pl.ds(GROUP * j, GROUP)
        return pltpu.make_async_copy(out_trc.at[:, layers], to_trc.at[:, layers], sems.at[4 + j])

    substep(trc, 0, lat_n, lat_s, put_first, lambda j: None)
    substep(c1, NF + 4, l1n, l1s, put_last, lambda j: leave(j).start())
    for move in leaving:
        move.wait()
    for j in range(K // GROUP):
        leave(j).wait()


def row_below(hyd, row, sub):
    rho = density(layer_rows(hyd, 0, row), layer_rows(hyd, K, row))
    return jnp.where(sub < K - 1, pltpu.roll(rho, K - 1, 0) - rho, 0.0)


def rate_table(after, rr, out):
    for t in range(NTR):
        for s in range(NTR):
            out[pl.ds((t * NTR + s) * ROWS, ROWS), :] = jnp.full((ROWS, COLS), SUB * rr[t, s])


def near(*dims):
    return pltpu.VMEM(dims, F32)


def far(*dims):
    return jax.ShapeDtypeStruct(dims, F32)


def held(x):
    return pltpu.with_memory_space_constraint(x, pltpu.VMEM)


def call(kernel, out_shape, spaces, scratch=(), flops=100000, out="v"):
    spec = {"a": pl.BlockSpec(memory_space=pl.ANY), "v": pl.BlockSpec(memory_space=pltpu.VMEM), "s": pl.BlockSpec(memory_space=pltpu.SMEM)}
    return pl.pallas_call(
        kernel,
        out_shape=out_shape,
        in_specs=[spec[c] for c in spaces],
        out_specs=tuple(spec[out] for _ in out_shape),
        scratch_shapes=list(scratch),
        cost_estimate=pl.CostEstimate(flops=flops, bytes_accessed=100000, transcendentals=0),
    )


def per_device(velocity, thickness, hydrography, tracers, land_mask, bottom_layer, row_biome, reaction_rates, growth_rates):
    lat, lon = lax.axis_size("lat"), lax.axis_size("lon")
    vel = velocity.reshape(2 * K * ROWS, COLS)
    thk = thickness.reshape(K * ROWS, COLS)
    hyd = hydrography.reshape(2 * K * ROWS, COLS)
    trc = tracers.reshape(NTR * K * ROWS, COLS)

    def swap(n, start):
        return [p for i in range(start, n - 1, 2) for p in ((i, i + 1), (i + 1, i))]

    *state, own = (held(x) for x in call(
        lon_pack,
        (near(2 * K * ROWS, COLS), near(K * ROWS, COLS), near(2 * K * ROWS, COLS), near(NTR * K * ROWS, COLS),
         near(ROWS, COLS), near(ROWS, COLS), near(PAIRS * ROWS, COLS)),
        "vvvvvvss",
    )(vel, thk, hyd, trc, land_mask, bottom_layer, row_biome, growth_rates))
    outer = held(lax.ppermute(own, "lon", swap(lon, 1)))
    inner = held(lax.ppermute(own, "lon", swap(lon, 0)))
    fwd, bwd = call(lat_pack, (near(C_FWD, COLS), near(C_BWD, COLS)), "vvvvv")(
        *state[:4], own)
    edge, fwd, bwd = call(
        edge_pack, (near(NF * ROWS, COLS), near(ROWS_FWD, COLS), near(ROWS_BWD, COLS)), "vvvvvvv"
    )(own, inner, outer, state[4], state[5], held(fwd), held(bwd))
    edge = held(edge)
    table = held(call(rate_table, (near(NTR * NTR * ROWS, COLS),), "vs")(edge, reaction_rates)[0])
    lat_s = held(lax.ppermute(fwd, "lat", [(i, i + 1) for i in range(lat - 1)]))
    lat_n = held(lax.ppermute(bwd, "lat", [(i + 1, i) for i in range(lat - 1)]))

    def body(*refs):
        step(lat * ROWS, *refs)

    outs = call(
        body,
        (far(2 * K * ROWS, COLS), far(K * ROWS, COLS), far(2 * K * ROWS, COLS), far(NTR, K, ROWS, COLS), far(K * ROWS, COLS)),
        "vvvvvvvvvv",
        out="a",
        scratch=[
            pltpu.VMEM((NF, 24, COLS), F32),
            pltpu.VMEM((4, 24, COLS), F32),
            pltpu.VMEM((NF + 4 + NTR, ROWS, COLS), F32),
            pltpu.VMEM((NTR * K, COLS), F32),
            pltpu.VMEM((NTR * K, COLS), F32),
            pltpu.VMEM((6, ROWS, COLS), F32),
            pltpu.VMEM((NTR * K * ROWS, COLS), F32),
            pltpu.VMEM((8, K * ROWS, COLS), F32),
            pltpu.VMEM((2 * K * ROWS, COLS), F32),
            pltpu.VMEM((K * ROWS, COLS), F32),
            pltpu.VMEM((2 * K * ROWS, COLS), F32),
            pltpu.VMEM((NTR, K, ROWS, COLS), F32),
            pltpu.VMEM((K * ROWS, COLS), F32),
            pltpu.SemaphoreType.DMA((4 + K // GROUP,)),
        ],
    )(*state, table, lat_s, lat_n, edge)
    new_vel, new_thk, new_hyd, new_trc, absorbed = outs
    return (new_vel.reshape(velocity.shape), new_thk.reshape(thickness.shape), new_hyd.reshape(hydrography.shape),
            new_trc.reshape(tracers.shape), absorbed.reshape(thickness.shape))


def solution(mesh):
    field = P(None, "lat", "lon")
    fields = P(None, None, "lat", "lon")
    in_specs = (fields, field, fields, fields, P("lat", "lon"), P("lat", "lon"), P("lat"), P(), P())
    out_specs = (fields, field, fields, fields, field)
    return jax.shard_map(per_device, mesh=mesh, in_specs=in_specs, out_specs=out_specs, check_vma=False)
```
